32 devices in a mesh: cell: 8 (over y, x, core), narrow: 4 (over z).
Axes of the slice: x: 2, y: 2, z: 4, core: 2. Of those that a mesh axis runs over, the one named last changes fastest.
Arguments:
- snapshots: bfloat16 [4096, 4096], P('cell', 'narrow'), may hold values from -6 to 6
- cell_volume: float32 [4096], P('cell'), may hold values from 0.1 to 10
- mode_vectors: bfloat16 [4096, 512], P('narrow'), may hold values from -0.09375 to 0.09375
- mode_scale: float32 [512], replicated, may hold values from 0.25 to 4
- interp_weights: bfloat16 [4096, 4096], P('cell', 'narrow'), may hold values from -0.09375 to 0.09375
Outputs:
- gram_matrix: float32 [4096, 4096], P('cell', 'narrow')
- fields: bfloat16 [4096, 4096], P('cell', 'narrow')
The draws below stay inside these ranges and needn't reach their ends.
All inputs are finite; a program needn't handle non-finite values.
Results may differ from the reference program's by a relative error of at most 0.0064.
Values may be sent and summed in bfloat16 or wider, within the bound.
A program may use at most 128 MiB of HBM per device.

```python
import math
import jax
import jax.numpy as jnp
from jax import lax

MODES = 512
CELLS = 4096
NSNAP = 4096
NCOND = 4096


def strengthened(drawn, key, source, target, shards_of, factor):
    def block_of(dim):
        return (jnp.arange(drawn.shape[dim]) // (drawn.shape[dim] // shards_of)).reshape((-1,) + (1,) * (drawn.ndim - 1 - dim))

    first = jax.random.permutation(key, shards_of)[block_of(target)]
    second = (block_of(target) + shards_of // 2) % shards_of
    return jnp.where((block_of(source) == first) | (block_of(source) == second), factor * drawn, drawn)


def block_levels(own_key, dims, split, low, top_value):
    factor_of = 1.0
    for position, blocks in split:
        steps = jax.random.uniform(jax.random.fold_in(jax.random.fold_in(own_key, 6), position), (blocks,), jnp.float32, low / len(split), top_value / len(split))
        factor_of = factor_of * jnp.repeat(jnp.exp(steps), dims[position] // blocks).reshape((-1,) + (1,) * (len(dims) - 1 - position))
    return factor_of


def gaussian(stream_key, shape, scale, most, split=(), dtype=jnp.bfloat16):
    factor_of = block_levels(stream_key, shape, split, -0.22, 0.18) if split else 1.0
    entries = jax.random.normal(stream_key, shape, jnp.float32) * scale * factor_of
    return jnp.minimum(jnp.maximum(entries, -most), most).astype(dtype)


def heavy_noise(rng, extent, spread, most, split, heavy, kind=jnp.bfloat16):
    entries = spread * jax.random.normal(rng, extent, jnp.float32)
    if split:
        entries = entries * block_levels(rng, extent, split, -0.22, 0.18)
    return jnp.clip(strengthened(entries, jax.random.fold_in(rng, 3), *heavy), -most, most).astype(kind)


def setup_inputs(seed: int = 0) -> dict:
    streams_of = jax.random.split(jax.random.key(seed), 6)
    return {
        "snapshots": heavy_noise(streams_of[0], (CELLS, NSNAP), 1.0, 6.0, ((0, 8), (1, 4)), (0, 1, 8, 2.0)),
        "cell_volume": jnp.clip(jnp.exp(math.log(10.0) - 4.6051702 * jax.random.uniform(streams_of[1], (CELLS,), jnp.float32) ** block_levels(streams_of[1], (CELLS,), ((0, 8),), -0.2, 0.2)), 0.1, 10.0),
        "mode_vectors": gaussian(streams_of[2], (NSNAP, MODES), NSNAP ** -0.5, 0.09375, ((0, 4),)),
        "mode_scale": jnp.clip(jnp.exp(jax.random.uniform(streams_of[3], (MODES,), jnp.float32, math.log(0.25), math.log(4.0))), 0.25, 4.0),
        "interp_weights": gaussian(streams_of[4], (NSNAP, NCOND), NSNAP ** -0.5, 0.09375, ((0, 8), (1, 4))),
    }


def reference(snapshots, cell_volume, mode_vectors, mode_scale, interp_weights):
    weighted = (snapshots.astype(jnp.float32) * cell_volume[:, None]).astype(jnp.bfloat16)
    gram_matrix = lax.dot_general(snapshots, weighted, (((0,), (0,)), ((), ())), preferred_element_type=jnp.float32) / CELLS
    summed = lax.dot_general(mode_vectors.astype(jnp.float32), gram_matrix, (((0,), (1,)), ((), ())), precision=lax.Precision.HIGHEST)
    coefficients = (mode_scale[:, None] * summed).astype(jnp.bfloat16)
    new_coeffs = jnp.dot(coefficients, interp_weights, preferred_element_type=jnp.float32).astype(jnp.bfloat16)
    mode_shapes = jnp.dot(snapshots, mode_vectors, preferred_element_type=jnp.float32).astype(jnp.bfloat16)
    fields = jnp.dot(mode_shapes, new_coeffs, preferred_element_type=jnp.float32).astype(jnp.bfloat16)
    return gram_matrix, fields
```

```python
import functools

import jax
import jax.numpy as jnp
from jax import lax
from jax.experimental import pallas as pl
from jax.experimental.pallas import tpu as pltpu
from jax.sharding import PartitionSpec as P

F32, BF16 = jnp.float32, jnp.bfloat16
MESH = pl.DeviceIdType.MESH
CHUNKS = 4
FAR = 4


def shards_xla(snapshots, cell_volume, mode_vectors, mode_scale, interp_weights):
    f32, bf16 = jnp.float32, jnp.bfloat16
    n_cell, n_narrow = lax.axis_size("cell"), lax.axis_size("narrow")
    total_cells = snapshots.shape[0] * n_cell
    rows = interp_weights.shape[0]
    weighted = (snapshots.astype(f32) * cell_volume[:, None]).astype(bf16)

    partial_shapes = jnp.dot(snapshots, mode_vectors, preferred_element_type=f32)
    mode_shapes = lax.psum(partial_shapes, "narrow").astype(bf16)

    gathered = lax.all_gather(snapshots, "narrow", axis=1, tiled=True)
    scaled_shapes = (
        mode_shapes.astype(f32) * (cell_volume / total_cells)[:, None] * mode_scale[None, :]
    ).astype(bf16)
    partial_coeffs = lax.dot_general(
        gathered, scaled_shapes, (((0,), (0,)), ((), ())), preferred_element_type=f32
    ).astype(bf16)
    coeffs = lax.psum_scatter(partial_coeffs, "cell", scatter_dimension=0, tiled=True)
    partial_new = lax.dot_general(
        coeffs, interp_weights, (((0,), (0,)), ((), ())), preferred_element_type=f32
    )
    new_coeffs = lax.psum(partial_new, "cell").astype(bf16)
    fields = jnp.dot(mode_shapes, new_coeffs, preferred_element_type=f32).astype(bf16)

    partial_gram = (
        lax.dot_general(gathered, weighted, (((0,), (0,)), ((), ())), preferred_element_type=f32)
        / total_cells
    ).astype(bf16)
    gram = lax.psum_scatter(partial_gram, "cell", scatter_dimension=0, tiled=True)
    return (gram.astype(f32), fields)


def pick(step, table, default):
    value = jnp.int32(default)
    for at, entry in table.items():
        value = jnp.where(step == at, jnp.int32(entry), value)
    return value


def kernel(
    C, Z, total, s, volb, v, scale, w, gram, fields,
    sg, sp, volp, vfull, wf, wfo, so, gsend, grecv, rrecv, gfar, ffar, frecv,
    mpart, msend, mout, mnear, mfar, mg, mgp, dm, csend, crecv, cown, kb, wq,
    nown, nsend, nrecv, ksend, krecv, kg,
    loc_sem, ps_sem, pr_sem, xs_sem, xr_sem, zs_sem, zr_sem, gs_sem, gr_sem, fs_sem, fr_sem,
    os_sem, or_sem, us_sem, ur_sem, hs_sem, hr_sem, m1s_sem, m1r_sem, m2s_sem, m2r_sem,
    cs_sem, cr_sem, bs_sem, br_sem, ws_sem, wr_sem, ks_sem, kr_sem, ls_sem, lr_sem, es_sem, er_sem,
):
    c, z = lax.axis_index("cell"), lax.axis_index("narrow")
    groups = C // 2
    p, k = c // 2, c % 2
    mate = 2 * p + 1 - k
    rows, cols = s.shape
    modes = v.shape[1]
    half = cols // 2
    cw = half // CHUNKS
    mrows = rows // CHUNKS
    hm = modes // 2

    low = z < Z // 2
    out = jnp.where(low, 0, Z - 1)
    inner = jnp.where(low, 1, Z - 2)
    inner2 = Z - 1 - inner
    out2 = Z - 1 - out
    edge = z == out
    mid = z != out
    inward = jnp.where(edge, inner, inner2)

    def remote(src, dst, ssem, rsem, cell, narrow):
        return pltpu.make_async_remote_copy(
            src_ref=src, dst_ref=dst, send_sem=ssem, recv_sem=rsem,
            device_id={"cell": cell, "narrow": narrow}, device_id_type=MESH,
        )

    def chip(d):
        return (p + d) % groups

    def plane(d):
        return (z + d) % Z

    barrier = pltpu.get_barrier_semaphore()

    def greet(cell, narrow):
        pl.semaphore_signal(
            barrier, inc=1, device_id={"cell": cell, "narrow": narrow}, device_id_type=MESH
        )

    greet(mate, z)
    for d in range(1, groups):
        greet(2 * chip(d) + k, z)
    for d in range(1, Z):
        greet(c, plane(d))
    pl.semaphore_wait(barrier, groups + Z - 1)

    mine = pl.ds(pl.multiple_of(k * rows, rows), rows)
    theirs = pl.ds(pl.multiple_of((1 - k) * rows, rows), rows)

    def local_copy(h):
        lanes = pl.ds(pl.multiple_of(k * half + h * cw, cw), cw)
        return pltpu.make_async_copy(s.at[:, lanes], sg.at[z, h, mine], loc_sem.at[h])

    def mate_copy(h):
        lanes = pl.ds(pl.multiple_of((1 - k) * half + h * cw, cw), cw)
        return remote(s.at[:, lanes], sg.at[z, h, mine], ps_sem.at[h], pr_sem.at[h], mate, z)

    def w_rows(q):
        return pl.ds(pl.multiple_of(q * mrows, mrows), mrows)

    def w_send(q):
        return remote(w.at[w_rows(q)], wq.at[p], ws_sem.at[q], wr_sem.at[p], 2 * q + k, z)

    def w_recv(q):
        return remote(w.at[w_rows(q)], wq.at[q], ws_sem.at[q], wr_sem.at[q], 2 * q + k, z)

    def in_copy(b, h):
        return remote(sg.at[b, h], sg.at[b, h], zs_sem.at[0, b, h], zr_sem.at[b, h], c, inward)

    def out_copy(b, h):
        return remote(sg.at[b, h], sg.at[b, h], zs_sem.at[1, b, h], zr_sem.at[b, h], c, out)

    def m_near(q):
        return remote(msend.at[q], mnear.at[q], m1s_sem.at[q], m1r_sem.at[q], c, inward)

    def m_far(q):
        return remote(msend.at[q], mfar.at[q], m1s_sem.at[q], m2r_sem.at[q], c, inward)

    def m_out(q):
        return remote(mout.at[q], mfar.at[q], m2s_sem.at[q], m2r_sem.at[q], c, out)

    block_copy = remote(s, sp, xs_sem.at[0], xr_sem.at[0], mate, z)
    vol_copy = remote(volb, volp, xs_sem.at[1], xr_sem.at[1], mate, z)
    mate_shapes = remote(mg, mgp, xs_sem.at[2], xr_sem.at[2], mate, z)
    new_half = remote(nsend, nrecv, xs_sem.at[3], xr_sem.at[3], mate, z)

    for h in range(CHUNKS):
        local_copy(h).start()
        mate_copy(h).start()
    vol_copy.start()
    block_copy.start()
    for d in (1, 2, 3):
        w_send(chip(d)).start()

    mpart[...] = jnp.dot(s[...], v[...], preferred_element_type=F32).reshape(mpart.shape)

    @pl.when(edge)
    def _():
        for q in range(CHUNKS):
            msend[q] = mpart[q].astype(BF16)
            m_near(q).start()

    for h in range(CHUNKS):
        local_copy(h).wait()
        mate_copy(h).wait_recv()

        @pl.when(edge)
        def _():
            in_copy(z, h).start()

        if h == 0:
            @pl.when(mid)
            def _():
                in_copy(z, h).start()

        if h < 2:
            @pl.when(mid)
            def _():
                out_copy(z, h).start()

    vfull[mine, :] = volb[...]
    wf[mine, :] = (s[...].astype(F32) * volb[:, :1]).astype(BF16)
    vol_copy.wait_recv()
    vfull[theirs, :] = volp[...]
    block_copy.wait_recv()
    wf[theirs, :] = (sp[...].astype(F32) * volp[:, :1]).astype(BF16)

    def apart(b):
        return jnp.where(p // 2 == b // 2, 0, 2) + jnp.where(p % 2 == b % 2, 0, 1)

    def flip(b, d):
        row = 1 - b // 2 if d == 2 else b // 2
        col = 1 - b % 2 if d == 1 else b % 2
        return 2 * row + col

    def direct(t, h, e, to):
        d = jnp.where(apart(to) == 1, 0, 1)
        r = jnp.where(t == FAR, CHUNKS, h)
        return remote(
            gsend.at[t, h, e], grecv.at[d, r, e], gs_sem.at[t, h, e], gr_sem.at[d, r, e],
            2 * to + k, z,
        )

    def across(t, h, e, to):
        return remote(
            gsend.at[t, h, e], rrecv.at[t, h], fs_sem.at[t, h, e], fr_sem.at[t, h],
            2 * flip(to, 1 if e == 0 else 2) + k, z,
        )

    def term(t, b, h, to, weights):
        value = lax.dot_general(
            sg[b, h], weights[...], (((0,), (0,)), ((), ())), preferred_element_type=F32
        ) * (1.0 / total)
        where = apart(to)

        @pl.when((where == 0) & (t != FAR))
        def _():
            gram[pl.ds(pl.multiple_of(h * cw, cw), cw), :] = value

        @pl.when((where == 0) & (t == FAR))
        def _():
            gfar[...] = value

        @pl.when(where != 0)
        def _():
            for e in range(2):
                gsend[t, h, e] = value[:, e * half:(e + 1) * half].astype(BF16)

        @pl.when(where == 3)
        def _():
            for e in range(2):
                across(t, h, e, to).start()

        @pl.when(where == 1)
        def _():
            direct(t, h, 1, to).start()

        @pl.when(where == 2)
        def _():
            direct(t, h, 0, to).start()

    def relay(t, h, to):
        where = apart(to)
        for e in range(2):
            @pl.when(where == e + 1)
            def _():
                across(t, h, e, to).wait_recv()
                gsend[t, h, e] = (
                    gsend[t, h, e].astype(F32) + rrecv[t, h].astype(F32)
                ).astype(BF16)
                direct(t, h, e, to).start()

    @pl.loop(0, CHUNKS)
    def _(h):
        term(z, z, h, z, wf)

    @pl.when(mid)
    def _():
        for q in range(CHUNKS):
            m_near(q).wait_recv()
            msend[q] = (mpart[q] + mnear[q].astype(F32)).astype(BF16)
            m_far(q).start()
        in_copy(z, 1).start()
        for q in range(CHUNKS):
            m_out(q).wait_recv()
            mine_far = mpart[q] + mfar[q].astype(F32)
            mout[q] = mine_far.astype(BF16)
            m_out(q).start()
            mg[q * mrows:(q + 1) * mrows, :] = (mine_far + mnear[q].astype(F32)).astype(BF16)
        out_copy(z, 2).start()
        out_copy(z, 3).start()

    def own_relay(h):
        relay(z, h, z)

    @pl.when(edge)
    def _():
        for q in range(CHUNKS):
            m_out(q).wait_recv()
            mg[q * mrows:(q + 1) * mrows, :] = (mpart[q] + mfar[q].astype(F32)).astype(BF16)

    mate_shapes.start()

    @pl.loop(0, CHUNKS)
    def _(h):
        own_relay(h)

    def o_copy(h):
        return remote(sg.at[out, h], so.at[h], os_sem.at[h], or_sem.at[h], mate, z)

    def o_weigh(block, h, core):
        lanes = pl.ds(pl.multiple_of(core * half + h * cw, cw), cw)
        wfo[:, lanes] = (block.astype(F32) * vfull[:, :1]).astype(BF16)

    def k_send(h):
        return remote(csend.at[h], crecv.at[p], cs_sem.at[h], cr_sem.at[p], 2 * h + k, z)

    def k_recv(q):
        return remote(csend.at[q], crecv.at[q], cs_sem.at[q], cr_sem.at[q], 2 * q + k, z)

    def k_share(t, b):
        return remote(kb.at[b], kb.at[b], bs_sem.at[t], br_sem.at[b], c, t)

    def n_send(q):
        return remote(ksend.at[q], krecv.at[p], ks_sem.at[q], kr_sem.at[p], 2 * q + k, z)

    def n_recv(q):
        return remote(ksend.at[q], krecv.at[q], ks_sem.at[q], kr_sem.at[q], 2 * q + k, z)

    def n_share(q, b):
        return remote(kg.at[k, b], kg.at[k, b], ls_sem.at[q], lr_sem.at[b], 2 * q + k, z)

    def n_mate(q, core):
        return remote(kg.at[core, q], kg.at[core, q], es_sem.at[q], er_sem.at[q], mate, z)

    def coefficients():
        mate_shapes.wait_recv()
        dm[mine, :] = (mg[...].astype(F32) * volb[:, :1]).astype(BF16)
        dm[theirs, :] = (mgp[...].astype(F32) * volp[:, :1]).astype(BF16)

        @pl.loop(0, CHUNKS)
        def _(h):
            value = lax.dot_general(
                sg[z, h], dm[...], (((0,), (0,)), ((), ())), preferred_element_type=F32
            )

            @pl.when(h == p)
            def _():
                cown[...] = value

            @pl.when(h != p)
            def _():
                csend[h] = value.astype(BF16)
                k_send(h).start()

    def coefficient_sum():
        value = cown[...]
        for d in (1, 2, 3):
            q = chip(d)
            k_recv(q).wait_recv()
            value = value + crecv[q].astype(F32)
        kb[z] = (value * (scale[...] * (1.0 / total))).astype(BF16)
        for d in (3, 2, 1):
            k_share(plane(d), z).start()

    def new_part():
        for d in (1, 2, 3):
            w_recv(chip(d)).wait_recv()
            k_share(plane(d), plane(d)).wait_recv()
        wq[p] = w[w_rows(p), :]
        value = lax.dot_general(
            kb[...].reshape(rows, modes), wq[...].reshape(rows, w.shape[1]),
            (((0,), (0,)), ((), ())), preferred_element_type=F32,
        )

        @pl.when(k == 0)
        def _():
            nown[...] = value[:hm]
            nsend[...] = value[hm:].astype(BF16)

        @pl.when(k == 1)
        def _():
            nown[...] = value[hm:]
            nsend[...] = value[:hm].astype(BF16)

        new_half.start()

    def new_scatter():
        new_half.wait_recv()
        value = nown[...] + nrecv[...].astype(F32)
        nown[...] = value
        ksend[...] = value.astype(BF16).reshape(ksend.shape)
        for d in (3, 1, 2):
            n_send(chip(d)).start()

    def new_sum():
        piece = hm // groups
        value = nown[pl.ds(pl.multiple_of(p * piece, piece), piece), :]
        for d in (1, 2, 3):
            q = chip(d)
            n_recv(q).wait_recv()
            value = value + krecv[q].astype(F32)
        kg[k, p] = value.astype(BF16)
        for d in (3, 1, 2):
            n_share(chip(d), p).start()
        n_mate(p, k).start()

    def new_gather():
        for d in (1, 2, 3):
            q = chip(d)
            n_share(q, q).wait_recv()
            n_mate(q, k).start()

    def reconstruct():
        for q in range(groups):
            n_mate(q, 1 - k).wait_recv()
        fields[...] = jnp.dot(
            mg[...], kg[...].reshape(modes, w.shape[1]), preferred_element_type=F32
        ).astype(BF16)

    def far_send():
        return remote(ffar, frecv.at[p], us_sem.at[0], ur_sem.at[p], c, out)

    def far_share(q):
        return remote(frecv.at[q], frecv.at[q], hs_sem.at[0], ur_sem.at[q], 2 * out2 + k, z)

    def far_sum():
        value = gfar[...]
        for d in range(2):
            for e in range(2):
                to = flip(p, d + 1)
                remote(
                    gsend.at[FAR, 0, e], grecv.at[d, CHUNKS, e], gs_sem.at[FAR, 0, e],
                    gr_sem.at[d, CHUNKS, e], 2 * to + k, z,
                ).wait_recv()
        parts = [
            (grecv[0, CHUNKS, e].astype(F32) + grecv[1, CHUNKS, e].astype(F32)) for e in range(2)
        ]
        ffar[...] = (value + jnp.concatenate(parts, axis=1)).astype(BF16)
        far_send().start()

    mid_steps = {
        4: (2, 0), 5: (1, 0), 6: (2, 1), 7: (1, 1), 8: (0, 0), 9: (1, 2), 10: (0, 1), 11: (1, 3),
        12: (4, 0), 13: (4, 1), 14: (0, 2), 15: (4, 2), 16: (0, 3), 17: (4, 3), 18: (2, 2), 19: (2, 3),
    }
    edge_steps = {
        4: (3, 0), 5: (3, 1), 6: (3, 2), 7: (3, 3), 10: (2, 0), 11: (2, 1), 18: (2, 2), 19: (2, 3),
    }

    def decode(step):
        kinds = [{at: entry[0] for at, entry in t.items()} for t in (mid_steps, edge_steps)]
        parts = [{at: entry[1] for at, entry in t.items()} for t in (mid_steps, edge_steps)]
        kind = jnp.where(edge, pick(step, kinds[1], -1), pick(step, kinds[0], -1))
        h = jnp.where(edge, pick(step, parts[1], 0), pick(step, parts[0], 0))
        b = jnp.where(
            kind == 1, out, jnp.where(kind == 2, inner2, jnp.where(kind == 3, inner, out2))
        )
        t = jnp.where(kind == 4, FAR, b)
        to = jnp.where(kind == 4, h, b)
        return kind, h, b, t, to

    def relay_step(step):
        kind, h, b, t, to = decode(step)

        @pl.when(kind >= 0)
        def _():
            relay(t, h, to)

    def far_step(step):
        kind, h, b, t, to = decode(step)

        @pl.when((kind == 4) & (h == p))
        def _():
            far_sum()

    @pl.loop(4, 20)
    def _(step):
        kind, h, b, t, to = decode(step)

        @pl.when((kind >= 0) & (kind < 4))
        def _():
            in_copy(b, h).wait_recv()

            @pl.when(mid & (kind == 1))
            def _():
                in_copy(b, h).start()
                o_copy(h).start()

            @pl.when(mid & (kind == 2))
            def _():
                out_copy(b, h).start()

            @pl.when(mid & (step == 11))
            def _():
                in_copy(z, 2).start()
                in_copy(z, 3).start()

            term(t, b, h, to, wf)

            @pl.when(mid & (kind == 1))
            def _():
                o_weigh(sg[b, h], h, k)

        @pl.when(mid & (step == 12))
        def _():
            for q in range(CHUNKS):
                o_copy(q).wait_recv()
                o_weigh(so[q], q, 1 - k)

        @pl.when(kind == 4)
        def _():
            term(t, b, h, to, wfo)

        relay_step(step - 1)
        far_step(step - 2)

        @pl.when(step == 4)
        def _():
            coefficients()

        @pl.when(step == 9)
        def _():
            coefficient_sum()

        @pl.when(step == 14)
        def _():
            new_part()

        @pl.when(step == 15)
        def _():
            new_scatter()

        @pl.when(step == 17)
        def _():
            new_sum()

        @pl.when(step == 18)
        def _():
            new_gather()

    relay_step(jnp.int32(19))

    @pl.when(edge & (p != out2))
    def _():
        far_send().wait_recv()
        far_share(p).start()

    reconstruct()

    @pl.when(mid | (p != out2))
    def _():
        @pl.loop(0, CHUNKS)
        def _(h):
            at = pl.ds(pl.multiple_of(h * cw, cw), cw)
            for d in range(2):
                to = flip(p, d + 1)
                for e in range(2):
                    remote(
                        gsend.at[p, h, e], grecv.at[d, h, e], gs_sem.at[p, h, e],
                        gr_sem.at[d, h, e], 2 * to + k, z,
                    ).wait_recv()
            for e in range(2):
                lanes = slice(e * half, (e + 1) * half)
                gram[at, lanes] = (
                    gram[at, lanes] + grecv[0, h, e].astype(F32) + grecv[1, h, e].astype(F32)
                )

    @pl.when(edge & (p == out2))
    def _():
        @pl.loop(0, CHUNKS)
        def _(h):
            remote(
                frecv.at[h], frecv.at[h], hs_sem.at[0], ur_sem.at[h], mate, z
            ).wait_recv()
            gram[pl.ds(pl.multiple_of(h * cw, cw), cw), :] = frecv[h].astype(F32)

    vol_copy.wait_send()
    block_copy.wait_send()
    mate_shapes.wait_send()
    new_half.wait_send()
    for h in range(CHUNKS):
        mate_copy(h).wait_send()
        m_near(h).wait_send()
        n_mate(h, k).wait_send()

        @pl.when(h != p)
        def _():
            k_send(h).wait_send()
    for d in (1, 2, 3):
        w_send(chip(d)).wait_send()
        n_send(chip(d)).wait_send()
        n_share(chip(d), p).wait_send()
        k_share(plane(d), z).wait_send()

    @pl.when(edge & (p != out2))
    def _():
        far_share(p).wait_send()

    def sent(t, h, to):
        where = apart(to)

        @pl.when((where == 1) | (where == 2))
        def _():
            for e in range(2):
                direct(t, h, e, to).wait_send()

        @pl.when(where == 3)
        def _():
            for e in range(2):
                across(t, h, e, to).wait_send()

    @pl.loop(0, CHUNKS)
    def _(h):
        in_copy(z, h).wait_send()
        for b in range(Z):
            @pl.when(mid | (b != out2))
            def _():
                sent(b, h, b)

        @pl.when(mid)
        def _():
            in_copy(out, h).wait_send()
            out_copy(z, h).wait_send()
            out_copy(inner2, h).wait_send()
            m_out(h).wait_send()
            o_copy(h).wait_send()
            sent(FAR, h, h)

    @pl.when(mid)
    def _():
        far_send().wait_send()


def shards_kernel(snapshots, cell_volume, mode_vectors, mode_scale, interp_weights):
    C, Z = lax.axis_size("cell"), lax.axis_size("narrow")
    groups = C // 2
    rows, cols = snapshots.shape
    modes = mode_vectors.shape[1]
    conds = interp_weights.shape[1]
    half = cols // 2
    cw = half // CHUNKS
    mrows = rows // CHUNKS
    hm = modes // 2
    dma = pltpu.SemaphoreType.DMA
    volb = jnp.broadcast_to(cell_volume[:, None], (rows, 128))
    vmem = pl.BlockSpec(memory_space=pltpu.VMEM)
    return pl.pallas_call(
        functools.partial(kernel, C, Z, rows * C),
        out_shape=(
            jax.ShapeDtypeStruct((half, cols), F32),
            jax.ShapeDtypeStruct((rows, conds), BF16),
        ),
        in_specs=[vmem] * 5,
        out_specs=(vmem, vmem),
        scratch_shapes=[
            pltpu.VMEM((Z, CHUNKS, 2 * rows, cw), BF16),
            pltpu.VMEM((rows, cols), BF16),
            pltpu.VMEM((rows, 128), F32),
            pltpu.VMEM((2 * rows, 128), F32),
            pltpu.VMEM((2 * rows, cols), BF16),
            pltpu.VMEM((2 * rows, cols), BF16),
            pltpu.VMEM((CHUNKS, 2 * rows, cw), BF16),
            pltpu.VMEM((FAR + 1, CHUNKS, 2, cw, half), BF16),
            pltpu.VMEM((2, CHUNKS + 1, 2, cw, half), BF16),
            pltpu.VMEM((FAR + 1, CHUNKS, cw, half), BF16),
            pltpu.VMEM((cw, cols), F32),
            pltpu.VMEM((cw, cols), BF16),
            pltpu.VMEM((CHUNKS, cw, cols), BF16),
            pltpu.VMEM((CHUNKS, mrows, modes), F32),
            pltpu.VMEM((CHUNKS, mrows, modes), BF16),
            pltpu.VMEM((CHUNKS, mrows, modes), BF16),
            pltpu.VMEM((CHUNKS, mrows, modes), BF16),
            pltpu.VMEM((CHUNKS, mrows, modes), BF16),
            pltpu.VMEM((rows, modes), BF16),
            pltpu.VMEM((rows, modes), BF16),
            pltpu.VMEM((2 * rows, modes), BF16),
            pltpu.VMEM((CHUNKS, cw, modes), BF16),
            pltpu.VMEM((CHUNKS, cw, modes), BF16),
            pltpu.VMEM((cw, modes), F32),
            pltpu.VMEM((Z, cw, modes), BF16),
            pltpu.VMEM((groups, mrows, conds), BF16),
            pltpu.VMEM((hm, conds), F32),
            pltpu.VMEM((hm, conds), BF16),
            pltpu.VMEM((hm, conds), BF16),
            pltpu.VMEM((groups, hm // groups, conds), BF16),
            pltpu.VMEM((groups, hm // groups, conds), BF16),
            pltpu.VMEM((2, groups, hm // groups, conds), BF16),
            dma((CHUNKS,)), dma((CHUNKS,)), dma((CHUNKS,)),
            dma((4,)), dma((4,)),
            dma((2, Z, CHUNKS)), dma((Z, CHUNKS)),
            dma((FAR + 1, CHUNKS, 2)), dma((2, CHUNKS + 1, 2)),
            dma((FAR + 1, CHUNKS, 2)), dma((FAR + 1, CHUNKS)),
            dma((CHUNKS,)), dma((CHUNKS,)),
            dma((1,)), dma((CHUNKS,)), dma((1,)), dma((1,)),
            dma((CHUNKS,)), dma((CHUNKS,)), dma((CHUNKS,)), dma((CHUNKS,)),
            dma((CHUNKS,)), dma((CHUNKS,)), dma((Z,)), dma((Z,)),
            dma((groups,)), dma((groups,)), dma((groups,)), dma((groups,)),
            dma((groups,)), dma((groups,)), dma((groups,)), dma((groups,)),
        ],
        compiler_params=pltpu.CompilerParams(
            collective_id=0, has_side_effects=True, vmem_limit_bytes=52 * 1024 * 1024
        ),
    )(snapshots, volb, mode_vectors, mode_scale[None, :], interp_weights)


def shards(snapshots, cell_volume, mode_vectors, mode_scale, interp_weights):
    C, Z = lax.axis_size("cell"), lax.axis_size("narrow")
    rows, cols = snapshots.shape
    modes = mode_vectors.shape[1]
    fits = (
        C == 2 * Z == 8
        and C == 2 * CHUNKS
        and cols % (2 * 128 * CHUNKS) == 0
        and rows % (16 * Z) == 0
        and modes % (16 * C) == 0
        and interp_weights.shape[0] == rows == cols // 2
        and rows * cols <= 512 * 1024
        and interp_weights.shape[1] <= 1024
        and modes <= 512
    )
    run = shards_kernel if fits else shards_xla
    return run(snapshots, cell_volume, mode_vectors, mode_scale, interp_weights)


def solution(mesh):
    return jax.shard_map(
        shards,
        mesh=mesh,
        in_specs=(P("cell", "narrow"), P("cell"), P("narrow", None), P(), P("cell", "narrow")),
        out_specs=(P("cell", "narrow"), P("cell", "narrow")),
        check_vma=False,
    )
```

```python
import functools

import jax
import jax.numpy as jnp
from jax import lax
from jax.experimental import pallas as pl
from jax.experimental.pallas import tpu as pltpu
from jax.sharding import PartitionSpec as P

F32, BF16 = jnp.float32, jnp.bfloat16
MESH = pl.DeviceIdType.MESH
CHUNKS = 4
FAR = 4
EARLY = 2


def shards_xla(snapshots, cell_volume, mode_vectors, mode_scale, interp_weights):
    f32, bf16 = jnp.float32, jnp.bfloat16
    n_cell, n_narrow = lax.axis_size("cell"), lax.axis_size("narrow")
    total_cells = snapshots.shape[0] * n_cell
    rows = interp_weights.shape[0]
    weighted = (snapshots.astype(f32) * cell_volume[:, None]).astype(bf16)

    partial_shapes = jnp.dot(snapshots, mode_vectors, preferred_element_type=f32)
    mode_shapes = lax.psum(partial_shapes, "narrow").astype(bf16)

    gathered = lax.all_gather(snapshots, "narrow", axis=1, tiled=True)
    scaled_shapes = (
        mode_shapes.astype(f32) * (cell_volume / total_cells)[:, None] * mode_scale[None, :]
    ).astype(bf16)
    partial_coeffs = lax.dot_general(
        gathered, scaled_shapes, (((0,), (0,)), ((), ())), preferred_element_type=f32
    ).astype(bf16)
    coeffs = lax.psum_scatter(partial_coeffs, "cell", scatter_dimension=0, tiled=True)
    partial_new = lax.dot_general(
        coeffs, interp_weights, (((0,), (0,)), ((), ())), preferred_element_type=f32
    )
    new_coeffs = lax.psum(partial_new, "cell").astype(bf16)
    fields = jnp.dot(mode_shapes, new_coeffs, preferred_element_type=f32).astype(bf16)

    partial_gram = (
        lax.dot_general(gathered, weighted, (((0,), (0,)), ((), ())), preferred_element_type=f32)
        / total_cells
    ).astype(bf16)
    gram = lax.psum_scatter(partial_gram, "cell", scatter_dimension=0, tiled=True)
    return (gram.astype(f32), fields)


def pick(step, table, default):
    value = jnp.int32(default)
    for at, entry in table.items():
        value = jnp.where(step == at, jnp.int32(entry), value)
    return value


def kernel(
    C, Z, total, s, volb, v, scale, w, gram, fields,
    sg, sp, volp, vfull, wf, wfo, so, gsend, grecv, rrecv, gfar, ffar, frecv,
    mpart, msend, mout, mnear, mfar, mg, dm, csend, crecv, cown, kb, wq,
    nown, nsend, nrecv, ksend, krecv, kg,
    loc_sem, ps_sem, pr_sem, xs_sem, xr_sem, zs_sem, zr_sem, gs_sem, gr_sem, fs_sem, fr_sem,
    os_sem, or_sem, us_sem, ur_sem, hs_sem, hr_sem, m1s_sem, m1r_sem, m2s_sem, m2r_sem,
    cs_sem, cr_sem, bs_sem, br_sem, ws_sem, wr_sem, ks_sem, kr_sem, ls_sem, lr_sem, es_sem, er_sem, ds_sem, dr_sem,
):
    c, z = lax.axis_index("cell"), lax.axis_index("narrow")
    groups = C // 2
    p, k = c // 2, c % 2
    mate = 2 * p + 1 - k
    rows, cols = s.shape
    modes = v.shape[1]
    half = cols // 2
    cw = half // CHUNKS
    mrows = rows // CHUNKS
    hm = modes // 2

    low = z < Z // 2
    out = jnp.where(low, 0, Z - 1)
    inner = jnp.where(low, 1, Z - 2)
    inner2 = Z - 1 - inner
    out2 = Z - 1 - out
    edge = z == out
    mid = z != out
    inward = jnp.where(edge, inner, inner2)

    def remote(src, dst, ssem, rsem, cell, narrow):
        return pltpu.make_async_remote_copy(
            src_ref=src, dst_ref=dst, send_sem=ssem, recv_sem=rsem,
            device_id={"cell": cell, "narrow": narrow}, device_id_type=MESH,
        )

    def chip(d):
        return (p + d) % groups

    def plane(d):
        return (z + d) % Z

    barrier = pltpu.get_barrier_semaphore()

    def greet(cell, narrow):
        pl.semaphore_signal(
            barrier, inc=1, device_id={"cell": cell, "narrow": narrow}, device_id_type=MESH
        )

    greet(mate, z)
    for d in range(1, groups):
        greet(2 * chip(d) + k, z)
    for d in range(1, Z):
        greet(c, plane(d))
    pl.semaphore_wait(barrier, groups + Z - 1)

    mine = pl.ds(pl.multiple_of(k * rows, rows), rows)
    theirs = pl.ds(pl.multiple_of((1 - k) * rows, rows), rows)

    def local_copy(h):
        lanes = pl.ds(pl.multiple_of(k * half + h * cw, cw), cw)
        return pltpu.make_async_copy(s.at[:, lanes], sg.at[z, h, mine], loc_sem.at[h])

    def mate_copy(h):
        lanes = pl.ds(pl.multiple_of((1 - k) * half + h * cw, cw), cw)
        return remote(s.at[:, lanes], sg.at[z, h, mine], ps_sem.at[h], pr_sem.at[h], mate, z)

    def w_rows(q):
        return pl.ds(pl.multiple_of(q * mrows, mrows), mrows)

    def w_send(q):
        return remote(w.at[w_rows(q)], wq.at[p], ws_sem.at[q], wr_sem.at[p], 2 * q + k, z)

    def w_recv(q):
        return remote(w.at[w_rows(q)], wq.at[q], ws_sem.at[q], wr_sem.at[q], 2 * q + k, z)

    def in_copy(b, h):
        return remote(sg.at[b, h], sg.at[b, h], zs_sem.at[0, b, h], zr_sem.at[b, h], c, inward)

    def out_copy(b, h):
        return remote(sg.at[b, h], sg.at[b, h], zs_sem.at[1, b, h], zr_sem.at[b, h], c, out)

    def m_near(q):
        return remote(msend.at[q], mnear.at[q], m1s_sem.at[q], m1r_sem.at[q], c, inward)

    def m_far(q):
        return remote(msend.at[q], mfar.at[q], m1s_sem.at[q], m2r_sem.at[q], c, inward)

    def m_out(q):
        return remote(mout.at[q], mfar.at[q], m2s_sem.at[q], m2r_sem.at[q], c, out)

    block_copy = remote(s, sp, xs_sem.at[0], xr_sem.at[0], mate, z)
    vol_copy = remote(volb, volp, xs_sem.at[1], xr_sem.at[1], mate, z)
    new_half = remote(nsend, nrecv, xs_sem.at[2], xr_sem.at[2], mate, z)

    def d_rows(q):
        return pl.ds(pl.multiple_of(k * rows + q * mrows, mrows), mrows)

    def d_copy(q):
        return remote(dm.at[d_rows(q)], dm.at[d_rows(q)], ds_sem.at[q], dr_sem.at[q], mate, z)

    def shape(q, value):
        mg[q * mrows:(q + 1) * mrows, :] = value.astype(BF16)
        dm[d_rows(q), :] = (value * volb[q * mrows:(q + 1) * mrows, :1]).astype(BF16)
        d_copy(q).start()

    for h in range(CHUNKS):
        local_copy(h).start()
        mate_copy(h).start()
    vol_copy.start()
    block_copy.start()
    for d in (1, 2, 3):
        w_send(chip(d)).start()

    mpart[...] = jnp.dot(s[...], v[...], preferred_element_type=F32).reshape(mpart.shape)

    @pl.when(edge)
    def _():
        for q in range(CHUNKS):
            msend[q] = mpart[q].astype(BF16)
            m_near(q).start()

    for h in range(CHUNKS):
        local_copy(h).wait()
        mate_copy(h).wait_recv()

        @pl.when(edge)
        def _():
            in_copy(z, h).start()

        if h == 0:
            @pl.when(mid)
            def _():
                in_copy(z, h).start()

        if h < 2:
            @pl.when(mid)
            def _():
                out_copy(z, h).start()

    vfull[mine, :] = volb[...]
    wf[mine, :] = (s[...].astype(F32) * volb[:, :1]).astype(BF16)
    vol_copy.wait_recv()
    vfull[theirs, :] = volp[...]
    block_copy.wait_recv()
    wf[theirs, :] = (sp[...].astype(F32) * volp[:, :1]).astype(BF16)

    def apart(b):
        return jnp.where(p // 2 == b // 2, 0, 2) + jnp.where(p % 2 == b % 2, 0, 1)

    def flip(b, d):
        row = 1 - b // 2 if d == 2 else b // 2
        col = 1 - b % 2 if d == 1 else b % 2
        return 2 * row + col

    def direct(t, h, e, to):
        d = jnp.where(apart(to) == 1, 0, 1)
        r = jnp.where(t == FAR, CHUNKS, h)
        return remote(
            gsend.at[t, h, e], grecv.at[d, r, e], gs_sem.at[t, h, e], gr_sem.at[d, r, e],
            2 * to + k, z,
        )

    def across(t, h, e, to):
        return remote(
            gsend.at[t, h, e], rrecv.at[t, h], fs_sem.at[t, h, e], fr_sem.at[t, h],
            2 * flip(to, 1 if e == 0 else 2) + k, z,
        )

    def term(t, b, h, to, weights):
        value = lax.dot_general(
            sg[b, h], weights[...], (((0,), (0,)), ((), ())), preferred_element_type=F32
        ) * (1.0 / total)
        where = apart(to)

        @pl.when((where == 0) & (t != FAR))
        def _():
            gram[pl.ds(pl.multiple_of(h * cw, cw), cw), :] = value

        @pl.when((where == 0) & (t == FAR))
        def _():
            gfar[...] = value

        @pl.when(where != 0)
        def _():
            for e in range(2):
                gsend[t, h, e] = value[:, e * half:(e + 1) * half].astype(BF16)

        @pl.when(where == 3)
        def _():
            for e in range(2):
                across(t, h, e, to).start()

        @pl.when(where == 1)
        def _():
            direct(t, h, 1, to).start()

        @pl.when(where == 2)
        def _():
            direct(t, h, 0, to).start()

    def relay(t, h, to):
        where = apart(to)
        for e in range(2):
            @pl.when(where == e + 1)
            def _():
                across(t, h, e, to).wait_recv()
                gsend[t, h, e] = (
                    gsend[t, h, e].astype(F32) + rrecv[t, h].astype(F32)
                ).astype(BF16)
                direct(t, h, e, to).start()

    @pl.loop(0, EARLY)
    def _(h):
        term(z, z, h, z, wf)

    @pl.when(edge)
    def _():
        @pl.loop(0, 2)
        def _(h):
            in_copy(inner, h).wait_recv()
            term(inner, inner, h, inner, wf)

    def near(q):
        m_near(q).wait_recv()
        msend[q] = (mpart[q] + mnear[q].astype(F32)).astype(BF16)
        m_far(q).start()

    def far(q):
        m_out(q).wait_recv()
        value = mpart[q] + mfar[q].astype(F32)
        mout[q] = value.astype(BF16)
        m_out(q).start()
        shape(q, value + mnear[q].astype(F32))

    @pl.when(mid)
    def _():
        near(0)
        near(1)
        near(2)
        far(0)
        near(3)
        in_copy(z, 1).start()
        far(1)
        far(2)
        far(3)
        out_copy(z, 2).start()
        out_copy(z, 3).start()

    @pl.when(edge)
    def _():
        for q in range(CHUNKS):
            m_out(q).wait_recv()
            shape(q, mpart[q] + mfar[q].astype(F32))

    def o_copy(h):
        return remote(sg.at[out, h], so.at[h], os_sem.at[h], or_sem.at[h], mate, z)

    def o_weigh(block, h, core):
        lanes = pl.ds(pl.multiple_of(core * half + h * cw, cw), cw)
        wfo[:, lanes] = (block.astype(F32) * vfull[:, :1]).astype(BF16)

    def k_send(h):
        return remote(csend.at[h], crecv.at[p], cs_sem.at[h], cr_sem.at[p], 2 * h + k, z)

    def k_recv(q):
        return remote(csend.at[q], crecv.at[q], cs_sem.at[q], cr_sem.at[q], 2 * q + k, z)

    def k_share(t, b):
        return remote(kb.at[b], kb.at[b], bs_sem.at[t], br_sem.at[b], c, t)

    def n_send(q):
        return remote(ksend.at[q], krecv.at[p], ks_sem.at[q], kr_sem.at[p], 2 * q + k, z)

    def n_recv(q):
        return remote(ksend.at[q], krecv.at[q], ks_sem.at[q], kr_sem.at[q], 2 * q + k, z)

    def n_share(q, b):
        return remote(kg.at[k, b], kg.at[k, b], ls_sem.at[q], lr_sem.at[b], 2 * q + k, z)

    def n_mate(q, core):
        return remote(kg.at[core, q], kg.at[core, q], es_sem.at[q], er_sem.at[q], mate, z)

    def coefficients():
        for q in range(CHUNKS):
            d_copy(q).wait_recv()

        @pl.loop(0, CHUNKS)
        def _(h):
            value = lax.dot_general(
                sg[z, h], dm[...], (((0,), (0,)), ((), ())), preferred_element_type=F32
            )

            @pl.when(h == p)
            def _():
                cown[...] = value

            @pl.when(h != p)
            def _():
                csend[h] = value.astype(BF16)
                k_send(h).start()

    def coefficient_sum():
        value = cown[...]
        for d in (1, 2, 3):
            q = chip(d)
            k_recv(q).wait_recv()
            value = value + crecv[q].astype(F32)
        kb[z] = (value * (scale[...] * (1.0 / total))).astype(BF16)
        for d in (3, 2, 1):
            k_share(plane(d), z).start()

    def new_part():
        for d in (1, 2, 3):
            w_recv(chip(d)).wait_recv()
            k_share(plane(d), plane(d)).wait_recv()
        wq[p] = w[w_rows(p), :]
        value = lax.dot_general(
            kb[...].reshape(rows, modes), wq[...].reshape(rows, w.shape[1]),
            (((0,), (0,)), ((), ())), preferred_element_type=F32,
        )

        @pl.when(k == 0)
        def _():
            nown[...] = value[:hm]
            nsend[...] = value[hm:]

        @pl.when(k == 1)
        def _():
            nown[...] = value[hm:]
            nsend[...] = value[:hm]

        new_half.start()

    def new_scatter():
        new_half.wait_recv()
        value = nown[...] + nrecv[...]
        nown[...] = value
        ksend[...] = value.astype(BF16).reshape(ksend.shape)
        for d in (3, 1, 2):
            n_send(chip(d)).start()

    def new_sum():
        piece = hm // groups
        value = nown[pl.ds(pl.multiple_of(p * piece, piece), piece), :]
        for d in (1, 2, 3):
            q = chip(d)
            n_recv(q).wait_recv()
            value = value + krecv[q].astype(F32)
        kg[k, p] = value.astype(BF16)
        for d in (3, 1, 2):
            n_share(chip(d), p).start()
        n_mate(p, k).start()

    def new_gather():
        for d in (1, 2, 3):
            q = chip(d)
            n_share(q, q).wait_recv()
            n_mate(q, k).start()

    def reconstruct():
        for q in range(groups):
            n_mate(q, 1 - k).wait_recv()
        fields[...] = jnp.dot(
            mg[...], kg[...].reshape(modes, w.shape[1]), preferred_element_type=F32
        ).astype(BF16)

    def far_send():
        return remote(ffar, frecv.at[p], us_sem.at[0], ur_sem.at[p], c, out)

    def far_share(q):
        return remote(frecv.at[q], frecv.at[q], hs_sem.at[0], ur_sem.at[q], 2 * out2 + k, z)

    def far_sum():
        value = gfar[...]
        for d in range(2):
            for e in range(2):
                to = flip(p, d + 1)
                remote(
                    gsend.at[FAR, 0, e], grecv.at[d, CHUNKS, e], gs_sem.at[FAR, 0, e],
                    gr_sem.at[d, CHUNKS, e], 2 * to + k, z,
                ).wait_recv()
        parts = [
            (grecv[0, CHUNKS, e].astype(F32) + grecv[1, CHUNKS, e].astype(F32)) for e in range(2)
        ]
        ffar[...] = (value + jnp.concatenate(parts, axis=1)).astype(BF16)
        far_send().start()

    OUT2, OUT, IN2, IN, ROWS = range(5)
    mid_terms = {
        0: (IN2, 0), 2: (OUT, 0), 3: (IN2, 1), 4: (OUT, 1), 5: (IN, 2), 6: (OUT2, 0), 7: (OUT, 2),
        8: (IN, 3), 9: (OUT, 3), 10: (OUT2, 1), 11: (ROWS, 0), 12: (ROWS, 1), 13: (OUT2, 2),
        14: (ROWS, 2), 16: (OUT2, 3), 17: (ROWS, 3), 18: (IN2, 2), 19: (IN2, 3),
    }
    mid_relays = {
        0: (IN, 0), 1: (IN, 1), 3: (IN2, 0), 5: (OUT, 0), 6: (IN2, 1), 7: (OUT, 1), 8: (IN, 2),
        10: (OUT2, 0), 11: (OUT, 2), 12: (OUT, 3), 13: (IN, 3), 14: (ROWS, 0), 15: (OUT2, 2),
        16: (ROWS, 2), 18: (OUT2, 3), 19: (ROWS, 3), 21: (IN2, 3),
    }
    mid_more = {13: (OUT2, 1), 14: (ROWS, 1), 19: (IN2, 2)}
    edge_terms = {
        4: (OUT, 2), 5: (OUT, 3), 6: (IN, 2), 7: (IN, 3), 9: (IN2, 0), 10: (IN2, 1), 18: (IN2, 2),
        20: (IN2, 3),
    }
    edge_relays = {
        0: (OUT, 0), 1: (OUT, 1), 2: (IN, 0), 3: (IN, 1), 6: (OUT, 2), 7: (OUT, 3), 8: (IN, 2),
        9: (IN, 3), 12: (IN2, 0), 14: (IN2, 1), 20: (IN2, 2), 21: (IN2, 3),
    }
    sums = {15: 0, 16: 1, 18: 2, 20: 3}
    STEPS = 22

    def decode(step, for_mid, for_edge):
        def code(table):
            return {at: 4 * entry[0] + entry[1] for at, entry in table.items()}

        event = jnp.where(edge, pick(step, code(for_edge), -4), pick(step, code(for_mid), -4))
        kind, h = (event + 4) // 4 - 1, (event + 4) % 4
        b = jnp.where(
            kind == OUT, out, jnp.where(kind == IN2, inner2, jnp.where(kind == IN, inner, out2))
        )
        t = jnp.where(kind == ROWS, FAR, b)
        to = jnp.where(kind == ROWS, h, b)
        return kind, h, b, t, to

    def relay_step(step, for_mid, for_edge):
        kind, h, b, t, to = decode(step, for_mid, for_edge)

        @pl.when(kind >= 0)
        def _():
            relay(t, h, to)

    @pl.loop(0, STEPS)
    def _(step):
        kind, h, b, t, to = decode(step, mid_terms, edge_terms)

        @pl.when((kind >= 0) & (kind != ROWS))
        def _():
            @pl.when(b != z)
            def _():
                in_copy(b, h).wait_recv()

            @pl.when(mid & (kind == OUT))
            def _():
                in_copy(b, h).start()
                o_copy(h).start()

            @pl.when(mid & (kind == IN2))
            def _():
                out_copy(b, h).start()

            @pl.when(mid & (kind == OUT) & (h == CHUNKS - 1))
            def _():
                in_copy(z, 2).start()
                in_copy(z, 3).start()

            term(t, b, h, to, wf)

            @pl.when(mid & (kind == OUT))
            def _():
                o_weigh(sg[b, h], h, k)

        @pl.when(mid & (step == 11))
        def _():
            for q in range(CHUNKS):
                o_copy(q).wait_recv()
                o_weigh(so[q], q, 1 - k)

        @pl.when(kind == ROWS)
        def _():
            term(t, b, h, to, wfo)

        relay_step(step, mid_relays, edge_relays)
        relay_step(step, mid_more, {})

        @pl.when(mid & (p == pick(step, sums, -1)))
        def _():
            far_sum()

        @pl.when(step == 1)
        def _():
            coefficients()

        @pl.when(step == 5)
        def _():
            coefficient_sum()

        @pl.when(step == 14)
        def _():
            new_part()

        @pl.when(step == 15)
        def _():
            new_scatter()

        @pl.when(step == 18)
        def _():
            new_sum()

        @pl.when(step == 20)
        def _():
            new_gather()

        @pl.when(edge & (p != out2) & (step == jnp.where(p >= groups // 2, STEPS - 1, STEPS - 3)))
        def _():
            far_send().wait_recv()
            far_share(p).start()

    reconstruct()

    @pl.when(mid | (p != out2))
    def _():
        @pl.loop(0, CHUNKS)
        def _(h):
            at = pl.ds(pl.multiple_of(h * cw, cw), cw)
            for d in range(2):
                to = flip(p, d + 1)
                for e in range(2):
                    remote(
                        gsend.at[p, h, e], grecv.at[d, h, e], gs_sem.at[p, h, e],
                        gr_sem.at[d, h, e], 2 * to + k, z,
                    ).wait_recv()
            for e in range(2):
                lanes = slice(e * half, (e + 1) * half)
                gram[at, lanes] = (
                    gram[at, lanes] + grecv[0, h, e].astype(F32) + grecv[1, h, e].astype(F32)
                )

    @pl.when(edge & (p == out2))
    def _():
        @pl.loop(0, CHUNKS)
        def _(h):
            remote(
                frecv.at[h], frecv.at[h], hs_sem.at[0], ur_sem.at[h], mate, z
            ).wait_recv()
            gram[pl.ds(pl.multiple_of(h * cw, cw), cw), :] = frecv[h].astype(F32)

    vol_copy.wait_send()
    block_copy.wait_send()
    new_half.wait_send()
    for h in range(CHUNKS):
        mate_copy(h).wait_send()
        m_near(h).wait_send()
        n_mate(h, k).wait_send()
        d_copy(h).wait_send()

        @pl.when(h != p)
        def _():
            k_send(h).wait_send()
    for d in (1, 2, 3):
        w_send(chip(d)).wait_send()
        n_send(chip(d)).wait_send()
        n_share(chip(d), p).wait_send()
        k_share(plane(d), z).wait_send()

    @pl.when(edge & (p != out2))
    def _():
        far_share(p).wait_send()

    def sent(t, h, to):
        where = apart(to)

        @pl.when((where == 1) | (where == 2))
        def _():
            for e in range(2):
                direct(t, h, e, to).wait_send()

        @pl.when(where == 3)
        def _():
            for e in range(2):
                across(t, h, e, to).wait_send()

    @pl.loop(0, CHUNKS)
    def _(h):
        in_copy(z, h).wait_send()
        for b in range(Z):
            @pl.when(mid | (b != out2))
            def _():
                sent(b, h, b)

        @pl.when(mid)
        def _():
            in_copy(out, h).wait_send()
            out_copy(z, h).wait_send()
            out_copy(inner2, h).wait_send()
            m_out(h).wait_send()
            o_copy(h).wait_send()
            sent(FAR, h, h)

    @pl.when(mid)
    def _():
        far_send().wait_send()


def shards_kernel(snapshots, cell_volume, mode_vectors, mode_scale, interp_weights):
    C, Z = lax.axis_size("cell"), lax.axis_size("narrow")
    groups = C // 2
    rows, cols = snapshots.shape
    modes = mode_vectors.shape[1]
    conds = interp_weights.shape[1]
    half = cols // 2
    cw = half // CHUNKS
    mrows = rows // CHUNKS
    hm = modes // 2
    dma = pltpu.SemaphoreType.DMA
    volb = jnp.broadcast_to(cell_volume[:, None], (rows, 128))
    vmem = pl.BlockSpec(memory_space=pltpu.VMEM)
    return pl.pallas_call(
        functools.partial(kernel, C, Z, rows * C),
        out_shape=(
            jax.ShapeDtypeStruct((half, cols), F32),
            jax.ShapeDtypeStruct((rows, conds), BF16),
        ),
        in_specs=[vmem] * 5,
        out_specs=(vmem, vmem),
        scratch_shapes=[
            pltpu.VMEM((Z, CHUNKS, 2 * rows, cw), BF16),
            pltpu.VMEM((rows, cols), BF16),
            pltpu.VMEM((rows, 128), F32),
            pltpu.VMEM((2 * rows, 128), F32),
            pltpu.VMEM((2 * rows, cols), BF16),
            pltpu.VMEM((2 * rows, cols), BF16),
            pltpu.VMEM((CHUNKS, 2 * rows, cw), BF16),
            pltpu.VMEM((FAR + 1, CHUNKS, 2, cw, half), BF16),
            pltpu.VMEM((2, CHUNKS + 1, 2, cw, half), BF16),
            pltpu.VMEM((FAR + 1, CHUNKS, cw, half), BF16),
            pltpu.VMEM((cw, cols), F32),
            pltpu.VMEM((cw, cols), BF16),
            pltpu.VMEM((CHUNKS, cw, cols), BF16),
            pltpu.VMEM((CHUNKS, mrows, modes), F32),
            pltpu.VMEM((CHUNKS, mrows, modes), BF16),
            pltpu.VMEM((CHUNKS, mrows, modes), BF16),
            pltpu.VMEM((CHUNKS, mrows, modes), BF16),
            pltpu.VMEM((CHUNKS, mrows, modes), BF16),
            pltpu.VMEM((rows, modes), BF16),
            pltpu.VMEM((2 * rows, modes), BF16),
            pltpu.VMEM((CHUNKS, cw, modes), BF16),
            pltpu.VMEM((CHUNKS, cw, modes), BF16),
            pltpu.VMEM((cw, modes), F32),
            pltpu.VMEM((Z, cw, modes), BF16),
            pltpu.VMEM((groups, mrows, conds), BF16),
            pltpu.VMEM((hm, conds), F32),
            pltpu.VMEM((hm, conds), F32),
            pltpu.VMEM((hm, conds), F32),
            pltpu.VMEM((groups, hm // groups, conds), BF16),
            pltpu.VMEM((groups, hm // groups, conds), BF16),
            pltpu.VMEM((2, groups, hm // groups, conds), BF16),
            dma((CHUNKS,)), dma((CHUNKS,)), dma((CHUNKS,)),
            dma((3,)), dma((3,)),
            dma((2, Z, CHUNKS)), dma((Z, CHUNKS)),
            dma((FAR + 1, CHUNKS, 2)), dma((2, CHUNKS + 1, 2)),
            dma((FAR + 1, CHUNKS, 2)), dma((FAR + 1, CHUNKS)),
            dma((CHUNKS,)), dma((CHUNKS,)),
            dma((1,)), dma((CHUNKS,)), dma((1,)), dma((1,)),
            dma((CHUNKS,)), dma((CHUNKS,)), dma((CHUNKS,)), dma((CHUNKS,)),
            dma((CHUNKS,)), dma((CHUNKS,)), dma((Z,)), dma((Z,)),
            dma((groups,)), dma((groups,)), dma((groups,)), dma((groups,)),
            dma((groups,)), dma((groups,)), dma((groups,)), dma((groups,)),
            dma((CHUNKS,)), dma((CHUNKS,)),
        ],
        compiler_params=pltpu.CompilerParams(
            collective_id=0, has_side_effects=True, vmem_limit_bytes=52 * 1024 * 1024
        ),
    )(snapshots, volb, mode_vectors, mode_scale[None, :], interp_weights)


def shards(snapshots, cell_volume, mode_vectors, mode_scale, interp_weights):
    C, Z = lax.axis_size("cell"), lax.axis_size("narrow")
    rows, cols = snapshots.shape
    modes = mode_vectors.shape[1]
    fits = (
        C == 2 * Z == 8
        and C == 2 * CHUNKS
        and cols % (2 * 128 * CHUNKS) == 0
        and rows % (16 * Z) == 0
        and modes % (16 * C) == 0
        and interp_weights.shape[0] == rows == cols // 2
        and rows * cols <= 512 * 1024
        and interp_weights.shape[1] <= 1024
        and modes <= 512
    )
    run = shards_kernel if fits else shards_xla
    return run(snapshots, cell_volume, mode_vectors, mode_scale, interp_weights)


def solution(mesh):
    return jax.shard_map(
        shards,
        mesh=mesh,
        in_specs=(P("cell", "narrow"), P("cell"), P("narrow", None), P(), P("cell", "narrow")),
        out_specs=(P("cell", "narrow"), P("cell", "narrow")),
        check_vma=False,
    )
```

```python
import functools

import jax
import jax.numpy as jnp
from jax import lax
from jax.experimental import pallas as pl
from jax.experimental.pallas import tpu as pltpu
from jax.sharding import PartitionSpec as P

F32, BF16 = jnp.float32, jnp.bfloat16
MESH = pl.DeviceIdType.MESH
CHUNKS = 4
FAR = 4
EARLY = 2


def shards_xla(snapshots, cell_volume, mode_vectors, mode_scale, interp_weights):
    f32, bf16 = jnp.float32, jnp.bfloat16
    n_cell, n_narrow = lax.axis_size("cell"), lax.axis_size("narrow")
    total_cells = snapshots.shape[0] * n_cell
    rows = interp_weights.shape[0]
    weighted = (snapshots.astype(f32) * cell_volume[:, None]).astype(bf16)

    partial_shapes = jnp.dot(snapshots, mode_vectors, preferred_element_type=f32)
    mode_shapes = lax.psum(partial_shapes, "narrow").astype(bf16)

    gathered = lax.all_gather(snapshots, "narrow", axis=1, tiled=True)
    scaled_shapes = (
        mode_shapes.astype(f32) * (cell_volume / total_cells)[:, None] * mode_scale[None, :]
    ).astype(bf16)
    partial_coeffs = lax.dot_general(
        gathered, scaled_shapes, (((0,), (0,)), ((), ())), preferred_element_type=f32
    ).astype(bf16)
    coeffs = lax.psum_scatter(partial_coeffs, "cell", scatter_dimension=0, tiled=True)
    partial_new = lax.dot_general(
        coeffs, interp_weights, (((0,), (0,)), ((), ())), preferred_element_type=f32
    )
    new_coeffs = lax.psum(partial_new, "cell").astype(bf16)
    fields = jnp.dot(mode_shapes, new_coeffs, preferred_element_type=f32).astype(bf16)

    partial_gram = (
        lax.dot_general(gathered, weighted, (((0,), (0,)), ((), ())), preferred_element_type=f32)
        / total_cells
    ).astype(bf16)
    gram = lax.psum_scatter(partial_gram, "cell", scatter_dimension=0, tiled=True)
    return (gram.astype(f32), fields)


def pick(step, table, default):
    value = jnp.int32(default)
    for at, entry in table.items():
        value = jnp.where(step == at, jnp.int32(entry), value)
    return value


def kernel(
    C, Z, total, s_in, vrow_in, v_in, scale_in, w_in, gram, fields,
    s, vrow, v, scale, w, sg, sp, prow, vfull, wf, wfo, so, gsend, grecv, rrecv, gfar, ffar, frecv,
    mpart, msend, mout, mnear, mfar, mg, dm, csend, crecv, cown, kb, wq,
    nown, nsend, nrecv, ksend, krecv, kg,
    loc_sem, ps_sem, pr_sem, xs_sem, xr_sem, zs_sem, zr_sem, gs_sem, gr_sem, fs_sem, fr_sem,
    os_sem, or_sem, us_sem, ur_sem, hs_sem, hr_sem, m1s_sem, m1r_sem, m2s_sem, m2r_sem,
    cs_sem, cr_sem, bs_sem, br_sem, ws_sem, wr_sem, ks_sem, kr_sem, ls_sem, lr_sem, es_sem, er_sem, ds_sem, dr_sem, in_sem,
):
    c, z = lax.axis_index("cell"), lax.axis_index("narrow")
    groups = C // 2
    p, k = c // 2, c % 2
    mate = 2 * p + 1 - k
    rows, cols = s.shape
    modes = v.shape[1]
    half = cols // 2
    cw = half // CHUNKS
    mrows = rows // CHUNKS
    hm = modes // 2

    low = z < Z // 2
    out = jnp.where(low, 0, Z - 1)
    inner = jnp.where(low, 1, Z - 2)
    inner2 = Z - 1 - inner
    out2 = Z - 1 - out
    edge = z == out
    mid = z != out
    inward = jnp.where(edge, inner, inner2)

    def remote(src, dst, ssem, rsem, cell, narrow):
        return pltpu.make_async_remote_copy(
            src_ref=src, dst_ref=dst, send_sem=ssem, recv_sem=rsem,
            device_id={"cell": cell, "narrow": narrow}, device_id_type=MESH,
        )

    def rows_chip(h):
        return jnp.where(low, groups - 1 - h, h)

    def chip(d):
        return (p + d) % groups

    def plane(d):
        return (z + d) % Z

    loads = [
        pltpu.make_async_copy(source, target, in_sem.at[at])
        for at, (source, target) in enumerate(
            ((s_in, s), (v_in, v), (vrow_in, vrow), (w_in, w), (scale_in, scale))
        )
    ]
    for load in loads:
        load.start()

    barrier = pltpu.get_barrier_semaphore()

    def greet(cell, narrow):
        pl.semaphore_signal(
            barrier, inc=1, device_id={"cell": cell, "narrow": narrow}, device_id_type=MESH
        )

    greet(mate, z)
    for d in range(1, groups):
        greet(2 * chip(d) + k, z)
    for d in range(1, Z):
        greet(c, plane(d))
    pl.semaphore_wait(barrier, groups + Z - 1)

    mine = pl.ds(pl.multiple_of(k * rows, rows), rows)
    theirs = pl.ds(pl.multiple_of((1 - k) * rows, rows), rows)

    def local_copy(h):
        lanes = pl.ds(pl.multiple_of(k * half + h * cw, cw), cw)
        return pltpu.make_async_copy(s.at[:, lanes], sg.at[z, h, mine], loc_sem.at[h])

    def mate_copy(h):
        lanes = pl.ds(pl.multiple_of((1 - k) * half + h * cw, cw), cw)
        return remote(s.at[:, lanes], sg.at[z, h, mine], ps_sem.at[h], pr_sem.at[h], mate, z)

    def w_rows(q):
        return pl.ds(pl.multiple_of(q * mrows, mrows), mrows)

    def w_send(q):
        return remote(w.at[w_rows(q)], wq.at[p], ws_sem.at[q], wr_sem.at[p], 2 * q + k, z)

    def w_recv(q):
        return remote(w.at[w_rows(q)], wq.at[q], ws_sem.at[q], wr_sem.at[q], 2 * q + k, z)

    def in_copy(b, h):
        return remote(sg.at[b, h], sg.at[b, h], zs_sem.at[0, b, h], zr_sem.at[b, h], c, inward)

    def out_copy(b, h):
        return remote(sg.at[b, h], sg.at[b, h], zs_sem.at[1, b, h], zr_sem.at[b, h], c, out)

    def m_near(q):
        return remote(msend.at[q], mnear.at[q], m1s_sem.at[q], m1r_sem.at[q], c, inward)

    def m_far(q):
        return remote(msend.at[q], mfar.at[q], m1s_sem.at[q], m2r_sem.at[q], c, inward)

    def m_out(q):
        return remote(mout.at[q], mfar.at[q], m2s_sem.at[q], m2r_sem.at[q], c, out)

    block_copy = remote(s, sp, xs_sem.at[0], xr_sem.at[0], mate, z)
    vol_copy = remote(vrow, prow, xs_sem.at[1], xr_sem.at[1], mate, z)
    new_half = remote(nsend, nrecv, xs_sem.at[2], xr_sem.at[2], mate, z)

    def d_rows(q):
        return pl.ds(pl.multiple_of(k * rows + q * mrows, mrows), mrows)

    def d_copy(q):
        return remote(dm.at[d_rows(q)], dm.at[d_rows(q)], ds_sem.at[q], dr_sem.at[q], mate, z)

    def shape(q, value):
        mg[q * mrows:(q + 1) * mrows, :] = value.astype(BF16)
        dm[d_rows(q), :] = (value * vfull[d_rows(q), :1]).astype(BF16)
        d_copy(q).start()

    loads[0].wait()
    for h in range(CHUNKS):
        local_copy(h).start()
        mate_copy(h).start()
    block_copy.start()
    loads[2].wait()
    vol_copy.start()
    loads[3].wait()
    for d in (1, 2, 3):
        w_send(chip(d)).start()

    loads[1].wait()
    mpart[...] = jnp.dot(s[...], v[...], preferred_element_type=F32).reshape(mpart.shape)

    loads[4].wait()

    @pl.when(edge)
    def _():
        for q in range(CHUNKS):
            msend[q] = mpart[q].astype(BF16)
            m_near(q).start()

    for h in range(CHUNKS):
        local_copy(h).wait()
        mate_copy(h).wait_recv()

        @pl.when(edge)
        def _():
            in_copy(z, h).start()

        if h == 0:
            @pl.when(mid)
            def _():
                in_copy(z, h).start()

        if h < 2:
            @pl.when(mid)
            def _():
                out_copy(z, h).start()

    def column(row):
        return jnp.broadcast_to(row[...], (128, rows)).T

    vfull[mine, :] = column(vrow)
    wf[mine, :] = (s[...].astype(F32) * vfull[mine, :1]).astype(BF16)
    vol_copy.wait_recv()
    vfull[theirs, :] = column(prow)
    block_copy.wait_recv()
    wf[theirs, :] = (sp[...].astype(F32) * vfull[theirs, :1]).astype(BF16)

    def apart(b):
        return jnp.where(p // 2 == b // 2, 0, 2) + jnp.where(p % 2 == b % 2, 0, 1)

    def flip(b, d):
        row = 1 - b // 2 if d == 2 else b // 2
        col = 1 - b % 2 if d == 1 else b % 2
        return 2 * row + col

    def direct(t, h, e, to):
        d = jnp.where(apart(to) == 1, 0, 1)
        r = jnp.where(t == FAR, CHUNKS, h)
        return remote(
            gsend.at[t, h, e], grecv.at[d, r, e], gs_sem.at[t, h, e], gr_sem.at[d, r, e],
            2 * to + k, z,
        )

    def across(t, h, e, to):
        return remote(
            gsend.at[t, h, e], rrecv.at[t, h], fs_sem.at[t, h, e], fr_sem.at[t, h],
            2 * flip(to, 1 if e == 0 else 2) + k, z,
        )

    def term(t, b, h, to, weights):
        value = lax.dot_general(
            sg[b, h], weights[...], (((0,), (0,)), ((), ())), preferred_element_type=F32
        ) * (1.0 / total)
        where = apart(to)

        @pl.when((where == 0) & (t != FAR))
        def _():
            gram[pl.ds(pl.multiple_of(h * cw, cw), cw), :] = value

        @pl.when((where == 0) & (t == FAR))
        def _():
            gfar[...] = value

        @pl.when(where != 0)
        def _():
            for e in range(2):
                gsend[t, h, e] = value[:, e * half:(e + 1) * half].astype(BF16)

        @pl.when(where == 3)
        def _():
            for e in range(2):
                across(t, h, e, to).start()

        @pl.when(where == 1)
        def _():
            direct(t, h, 1, to).start()

        @pl.when(where == 2)
        def _():
            direct(t, h, 0, to).start()

    def relay(t, h, to):
        where = apart(to)
        for e in range(2):
            @pl.when(where == e + 1)
            def _():
                across(t, h, e, to).wait_recv()
                gsend[t, h, e] = (
                    gsend[t, h, e].astype(F32) + rrecv[t, h].astype(F32)
                ).astype(BF16)
                direct(t, h, e, to).start()

    @pl.when(mid)
    def _():
        @pl.loop(0, EARLY)
        def _(h):
            term(z, z, h, z, wf)

    @pl.when(edge)
    def _():
        @pl.loop(0, 2)
        def _(h):
            in_copy(inner, h).wait_recv()
            term(inner, inner, h, inner, wf)

    def near(q):
        m_near(q).wait_recv()
        msend[q] = (mpart[q] + mnear[q].astype(F32)).astype(BF16)
        m_far(q).start()

    def far(q):
        m_out(q).wait_recv()
        value = mpart[q] + mfar[q].astype(F32)
        mout[q] = value.astype(BF16)
        m_out(q).start()
        shape(q, value + mnear[q].astype(F32))

    @pl.when(mid)
    def _():
        near(0)
        near(1)
        near(2)
        far(0)
        near(3)
        in_copy(z, 1).start()
        far(1)
        far(2)
        far(3)
        out_copy(z, 2).start()
        out_copy(z, 3).start()

    @pl.when(edge)
    def _():
        for q in range(CHUNKS):
            m_out(q).wait_recv()
            shape(q, mpart[q] + mfar[q].astype(F32))

    def o_copy(h):
        return remote(sg.at[out, h], so.at[h], os_sem.at[h], or_sem.at[h], mate, z)

    def o_weigh(block, h, core):
        lanes = pl.ds(pl.multiple_of(core * half + h * cw, cw), cw)
        wfo[:, lanes] = (block.astype(F32) * vfull[:, :1]).astype(BF16)

    def k_send(h):
        return remote(csend.at[h], crecv.at[p], cs_sem.at[h], cr_sem.at[p], 2 * h + k, z)

    def k_recv(q):
        return remote(csend.at[q], crecv.at[q], cs_sem.at[q], cr_sem.at[q], 2 * q + k, z)

    def k_share(t, b):
        return remote(kb.at[b], kb.at[b], bs_sem.at[t], br_sem.at[b], c, t)

    def n_send(q):
        return remote(ksend.at[q], krecv.at[p], ks_sem.at[q], kr_sem.at[p], 2 * q + k, z)

    def n_recv(q):
        return remote(ksend.at[q], krecv.at[q], ks_sem.at[q], kr_sem.at[q], 2 * q + k, z)

    def n_share(q, b):
        return remote(kg.at[k, b], kg.at[k, b], ls_sem.at[q], lr_sem.at[b], 2 * q + k, z)

    def n_mate(q, core):
        return remote(kg.at[core, q], kg.at[core, q], es_sem.at[q], er_sem.at[q], mate, z)

    def coefficients():
        for q in range(CHUNKS):
            d_copy(q).wait_recv()

        @pl.loop(0, CHUNKS)
        def _(h):
            value = lax.dot_general(
                sg[z, h], dm[...], (((0,), (0,)), ((), ())), preferred_element_type=F32
            )

            @pl.when(h == p)
            def _():
                cown[...] = value

            @pl.when(h != p)
            def _():
                csend[h] = value.astype(BF16)
                k_send(h).start()

    def coefficient_sum():
        value = cown[...]
        for d in (1, 2, 3):
            q = chip(d)
            k_recv(q).wait_recv()
            value = value + crecv[q].astype(F32)
        kb[z] = (value * (scale[...] * (1.0 / total))).astype(BF16)
        for d in (3, 2, 1):
            k_share(plane(d), z).start()

    def new_part():
        for d in (1, 2, 3):
            w_recv(chip(d)).wait_recv()
            k_share(plane(d), plane(d)).wait_recv()
        wq[p] = w[w_rows(p), :]
        value = lax.dot_general(
            kb[...].reshape(rows, modes), wq[...].reshape(rows, w.shape[1]),
            (((0,), (0,)), ((), ())), preferred_element_type=F32,
        )

        @pl.when(k == 0)
        def _():
            nown[...] = value[:hm]
            nsend[...] = value[hm:]

        @pl.when(k == 1)
        def _():
            nown[...] = value[hm:]
            nsend[...] = value[:hm]

        new_half.start()

    def new_scatter():
        new_half.wait_recv()
        value = nown[...] + nrecv[...]
        nown[...] = value
        ksend[...] = value.astype(BF16).reshape(ksend.shape)
        for d in (3, 1, 2):
            n_send(chip(d)).start()

    def new_sum():
        piece = hm // groups
        value = nown[pl.ds(pl.multiple_of(p * piece, piece), piece), :]
        for d in (1, 2, 3):
            q = chip(d)
            n_recv(q).wait_recv()
            value = value + krecv[q].astype(F32)
        kg[k, p] = value.astype(BF16)
        for d in (3, 1, 2):
            n_share(chip(d), p).start()
        n_mate(p, k).start()

    def new_gather():
        for d in (1, 2, 3):
            q = chip(d)
            n_share(q, q).wait_recv()
            n_mate(q, k).start()

    def reconstruct():
        for q in range(groups):
            n_mate(q, 1 - k).wait_recv()
        fields[...] = jnp.dot(
            mg[...], kg[...].reshape(modes, w.shape[1]), preferred_element_type=F32
        ).astype(BF16)

    own_rows = rows_chip(p)

    def far_send():
        return remote(ffar, frecv.at[own_rows], us_sem.at[0], ur_sem.at[own_rows], c, out)

    def far_share(q):
        return remote(frecv.at[q], frecv.at[q], hs_sem.at[0], ur_sem.at[q], 2 * out2 + k, z)

    def far_sum():
        value = gfar[...]
        for d in range(2):
            for e in range(2):
                to = flip(p, d + 1)
                remote(
                    gsend.at[FAR, 0, e], grecv.at[d, CHUNKS, e], gs_sem.at[FAR, 0, e],
                    gr_sem.at[d, CHUNKS, e], 2 * to + k, z,
                ).wait_recv()
        parts = [
            (grecv[0, CHUNKS, e].astype(F32) + grecv[1, CHUNKS, e].astype(F32)) for e in range(2)
        ]
        ffar[...] = (value + jnp.concatenate(parts, axis=1)).astype(BF16)
        far_send().start()

    OUT2, OUT, IN2, IN, ROWS = range(5)
    mid_terms = {
        0: (IN2, 0), 2: (OUT, 0), 3: (IN2, 1), 4: (OUT, 1), 5: (IN, 2), 6: (OUT2, 0), 7: (OUT, 2),
        8: (IN, 3), 9: (OUT, 3), 10: (OUT2, 1), 11: (ROWS, 0), 12: (ROWS, 1), 13: (OUT2, 2),
        14: (ROWS, 2), 16: (OUT2, 3), 17: (ROWS, 3), 18: (IN2, 2), 19: (IN2, 3),
    }
    mid_relays = {
        0: (IN, 0), 1: (IN, 1), 3: (IN2, 0), 5: (OUT, 0), 6: (IN2, 1), 7: (OUT, 1), 8: (IN, 2),
        10: (OUT2, 0), 11: (OUT, 2), 12: (OUT, 3), 13: (IN, 3), 14: (ROWS, 0), 15: (OUT2, 2),
        16: (ROWS, 2), 19: (OUT2, 3), 20: (IN2, 2), 21: (IN2, 3),
    }
    mid_more = {13: (OUT2, 1), 14: (ROWS, 1), 19: (ROWS, 3)}
    edge_terms = {
        2: (OUT, 0), 3: (OUT, 1), 4: (OUT, 2), 5: (OUT, 3), 6: (IN, 2), 7: (IN, 3), 10: (IN2, 0),
        14: (IN2, 1), 18: (IN2, 2), 20: (IN2, 3),
    }
    edge_relays = {
        2: (IN, 0), 3: (IN, 1), 5: (OUT, 0), 6: (OUT, 1), 7: (OUT, 2), 8: (OUT, 3), 9: (IN, 2),
        10: (IN, 3), 14: (IN2, 0), 16: (IN2, 1), 20: (IN2, 2), 21: (IN2, 3),
    }
    STEPS = 22

    def decode(step, for_mid, for_edge):
        def code(table):
            return {at: 4 * entry[0] + entry[1] for at, entry in table.items()}

        event = jnp.where(edge, pick(step, code(for_edge), -4), pick(step, code(for_mid), -4))
        kind, h = (event + 4) // 4 - 1, (event + 4) % 4
        b = jnp.where(
            kind == OUT, out, jnp.where(kind == IN2, inner2, jnp.where(kind == IN, inner, out2))
        )
        t = jnp.where(kind == ROWS, FAR, b)
        to = jnp.where(kind == ROWS, rows_chip(h), b)
        return kind, h, b, t, to

    def relay_step(step, for_mid, for_edge):
        kind, h, b, t, to = decode(step, for_mid, for_edge)

        @pl.when(kind >= 0)
        def _():
            relay(t, h, to)

    @pl.loop(0, STEPS)
    def _(step):
        kind, h, b, t, to = decode(step, mid_terms, edge_terms)

        @pl.when((kind >= 0) & (kind != ROWS))
        def _():
            @pl.when(b != z)
            def _():
                in_copy(b, h).wait_recv()

            @pl.when(mid & (kind == OUT))
            def _():
                in_copy(b, h).start()
                o_copy(h).start()

            @pl.when(mid & (kind == IN2))
            def _():
                out_copy(b, h).start()

            @pl.when(mid & (kind == OUT) & (h == CHUNKS - 1))
            def _():
                in_copy(z, 2).start()
                in_copy(z, 3).start()

            term(t, b, h, to, wf)

            @pl.when(mid & (kind == OUT))
            def _():
                o_weigh(sg[b, h], h, k)

        @pl.when(mid & (step == 11))
        def _():
            for q in range(CHUNKS):
                o_copy(q).wait_recv()
                o_weigh(so[q], q, 1 - k)

        @pl.when(kind == ROWS)
        def _():
            term(t, b, h, to, wfo)

        @pl.when(step == 1)
        def _():
            coefficients()

        @pl.when(step == 5)
        def _():
            coefficient_sum()

        @pl.when(step == 12)
        def _():
            new_part()

        @pl.when(step == 13)
        def _():
            new_scatter()

        @pl.when(step == 17)
        def _():
            new_sum()

        @pl.when(step == 20)
        def _():
            new_gather()

        relay_step(step, mid_relays, edge_relays)
        relay_step(step, mid_more, {})

        @pl.when(mid & (step == 19 + own_rows // 2))
        def _():
            far_sum()

        @pl.when(edge & (p != out2) & (step == jnp.where(own_rows >= groups // 2, STEPS - 1, STEPS - 3)))
        def _():
            far_send().wait_recv()
            far_share(own_rows).start()

    reconstruct()

    @pl.when(mid | (p != out2))
    def _():
        @pl.loop(0, CHUNKS)
        def _(h):
            at = pl.ds(pl.multiple_of(h * cw, cw), cw)
            for d in range(2):
                to = flip(p, d + 1)
                for e in range(2):
                    remote(
                        gsend.at[p, h, e], grecv.at[d, h, e], gs_sem.at[p, h, e],
                        gr_sem.at[d, h, e], 2 * to + k, z,
                    ).wait_recv()
            for e in range(2):
                lanes = slice(e * half, (e + 1) * half)
                gram[at, lanes] = (
                    gram[at, lanes] + grecv[0, h, e].astype(F32) + grecv[1, h, e].astype(F32)
                )

    @pl.when(edge & (p == out2))
    def _():
        @pl.loop(0, CHUNKS)
        def _(h):
            remote(
                frecv.at[h], frecv.at[h], hs_sem.at[0], ur_sem.at[h], mate, z
            ).wait_recv()
            gram[pl.ds(pl.multiple_of(h * cw, cw), cw), :] = frecv[h].astype(F32)

    vol_copy.wait_send()
    block_copy.wait_send()
    new_half.wait_send()
    for h in range(CHUNKS):
        mate_copy(h).wait_send()
        m_near(h).wait_send()
        n_mate(h, k).wait_send()
        d_copy(h).wait_send()

        @pl.when(h != p)
        def _():
            k_send(h).wait_send()
    for d in (1, 2, 3):
        w_send(chip(d)).wait_send()
        n_send(chip(d)).wait_send()
        n_share(chip(d), p).wait_send()
        k_share(plane(d), z).wait_send()

    @pl.when(edge & (p != out2))
    def _():
        far_share(own_rows).wait_send()

    def sent(t, h, to):
        where = apart(to)

        @pl.when((where == 1) | (where == 2))
        def _():
            for e in range(2):
                direct(t, h, e, to).wait_send()

        @pl.when(where == 3)
        def _():
            for e in range(2):
                across(t, h, e, to).wait_send()

    @pl.loop(0, CHUNKS)
    def _(h):
        in_copy(z, h).wait_send()
        for b in range(Z):
            @pl.when(mid | (b != out2))
            def _():
                sent(b, h, b)

        @pl.when(mid)
        def _():
            in_copy(out, h).wait_send()
            out_copy(z, h).wait_send()
            out_copy(inner2, h).wait_send()
            m_out(h).wait_send()
            o_copy(h).wait_send()
            sent(FAR, h, rows_chip(h))

    @pl.when(mid)
    def _():
        far_send().wait_send()


def shards_kernel(snapshots, cell_volume, mode_vectors, mode_scale, interp_weights):
    C, Z = lax.axis_size("cell"), lax.axis_size("narrow")
    groups = C // 2
    rows, cols = snapshots.shape
    modes = mode_vectors.shape[1]
    conds = interp_weights.shape[1]
    half = cols // 2
    cw = half // CHUNKS
    mrows = rows // CHUNKS
    hm = modes // 2
    dma = pltpu.SemaphoreType.DMA
    vmem = pl.BlockSpec(memory_space=pltpu.VMEM)
    inputs = (snapshots, cell_volume[None, :], mode_vectors, mode_scale[None, :], interp_weights)
    inputs = [pltpu.with_memory_space_constraint(x, pltpu.HBM) for x in inputs]
    return pl.pallas_call(
        functools.partial(kernel, C, Z, rows * C),
        out_shape=(
            jax.ShapeDtypeStruct((half, cols), F32),
            jax.ShapeDtypeStruct((rows, conds), BF16),
        ),
        in_specs=[pl.BlockSpec(memory_space=pltpu.HBM)] * 5,
        out_specs=(vmem, vmem),
        scratch_shapes=[
            pltpu.VMEM((rows, cols), BF16),
            pltpu.VMEM((1, rows), F32),
            pltpu.VMEM((cols, modes), BF16),
            pltpu.VMEM((1, modes), F32),
            pltpu.VMEM((rows, conds), BF16),
            pltpu.VMEM((Z, CHUNKS, 2 * rows, cw), BF16),
            pltpu.VMEM((rows, cols), BF16),
            pltpu.VMEM((1, rows), F32),
            pltpu.VMEM((2 * rows, 128), F32),
            pltpu.VMEM((2 * rows, cols), BF16),
            pltpu.VMEM((2 * rows, cols), BF16),
            pltpu.VMEM((CHUNKS, 2 * rows, cw), BF16),
            pltpu.VMEM((FAR + 1, CHUNKS, 2, cw, half), BF16),
            pltpu.VMEM((2, CHUNKS + 1, 2, cw, half), BF16),
            pltpu.VMEM((FAR + 1, CHUNKS, cw, half), BF16),
            pltpu.VMEM((cw, cols), F32),
            pltpu.VMEM((cw, cols), BF16),
            pltpu.VMEM((CHUNKS, cw, cols), BF16),
            pltpu.VMEM((CHUNKS, mrows, modes), F32),
            pltpu.VMEM((CHUNKS, mrows, modes), BF16),
            pltpu.VMEM((CHUNKS, mrows, modes), BF16),
            pltpu.VMEM((CHUNKS, mrows, modes), BF16),
            pltpu.VMEM((CHUNKS, mrows, modes), BF16),
            pltpu.VMEM((rows, modes), BF16),
            pltpu.VMEM((2 * rows, modes), BF16),
            pltpu.VMEM((CHUNKS, cw, modes), BF16),
            pltpu.VMEM((CHUNKS, cw, modes), BF16),
            pltpu.VMEM((cw, modes), F32),
            pltpu.VMEM((Z, cw, modes), BF16),
            pltpu.VMEM((groups, mrows, conds), BF16),
            pltpu.VMEM((hm, conds), F32),
            pltpu.VMEM((hm, conds), F32),
            pltpu.VMEM((hm, conds), F32),
            pltpu.VMEM((groups, hm // groups, conds), BF16),
            pltpu.VMEM((groups, hm // groups, conds), BF16),
            pltpu.VMEM((2, groups, hm // groups, conds), BF16),
            dma((CHUNKS,)), dma((CHUNKS,)), dma((CHUNKS,)),
            dma((3,)), dma((3,)),
            dma((2, Z, CHUNKS)), dma((Z, CHUNKS)),
            dma((FAR + 1, CHUNKS, 2)), dma((2, CHUNKS + 1, 2)),
            dma((FAR + 1, CHUNKS, 2)), dma((FAR + 1, CHUNKS)),
            dma((CHUNKS,)), dma((CHUNKS,)),
            dma((1,)), dma((CHUNKS,)), dma((1,)), dma((1,)),
            dma((CHUNKS,)), dma((CHUNKS,)), dma((CHUNKS,)), dma((CHUNKS,)),
            dma((CHUNKS,)), dma((CHUNKS,)), dma((Z,)), dma((Z,)),
            dma((groups,)), dma((groups,)), dma((groups,)), dma((groups,)),
            dma((groups,)), dma((groups,)), dma((groups,)), dma((groups,)),
            dma((CHUNKS,)), dma((CHUNKS,)), dma((5,)),
        ],
        compiler_params=pltpu.CompilerParams(
            collective_id=0, has_side_effects=True, vmem_limit_bytes=45 * 1024 * 1024
        ),
    )(*inputs)


def shards(snapshots, cell_volume, mode_vectors, mode_scale, interp_weights):
    C, Z = lax.axis_size("cell"), lax.axis_size("narrow")
    rows, cols = snapshots.shape
    modes = mode_vectors.shape[1]
    fits = (
        C == 2 * Z == 8
        and C == 2 * CHUNKS
        and cols % (2 * 128 * CHUNKS) == 0
        and rows % (16 * Z) == 0
        and modes % (16 * C) == 0
        and interp_weights.shape[0] == rows == cols // 2
        and rows * cols <= 512 * 1024
        and interp_weights.shape[1] <= 1024
        and modes <= 512
    )
    run = shards_kernel if fits else shards_xla
    return run(snapshots, cell_volume, mode_vectors, mode_scale, interp_weights)


def solution(mesh):
    return jax.shard_map(
        shards,
        mesh=mesh,
        in_specs=(P("cell", "narrow"), P("cell"), P("narrow", None), P(), P("cell", "narrow")),
        out_specs=(P("cell", "narrow"), P("cell", "narrow")),
        check_vma=False,
    )
```

```python
import functools

import jax
import jax.numpy as jnp
from jax import lax
from jax.experimental import pallas as pl
from jax.experimental.pallas import tpu as pltpu
from jax.sharding import PartitionSpec as P

F32, BF16 = jnp.float32, jnp.bfloat16
MESH = pl.DeviceIdType.MESH
CHUNKS = 4
FAR = 4
EARLY = 2


def shards_xla(snapshots, cell_volume, mode_vectors, mode_scale, interp_weights):
    f32, bf16 = jnp.float32, jnp.bfloat16
    n_cell, n_narrow = lax.axis_size("cell"), lax.axis_size("narrow")
    total_cells = snapshots.shape[0] * n_cell
    rows = interp_weights.shape[0]
    weighted = (snapshots.astype(f32) * cell_volume[:, None]).astype(bf16)

    partial_shapes = jnp.dot(snapshots, mode_vectors, preferred_element_type=f32)
    mode_shapes = lax.psum(partial_shapes, "narrow").astype(bf16)

    gathered = lax.all_gather(snapshots, "narrow", axis=1, tiled=True)
    scaled_shapes = (
        mode_shapes.astype(f32) * (cell_volume / total_cells)[:, None] * mode_scale[None, :]
    ).astype(bf16)
    partial_coeffs = lax.dot_general(
        gathered, scaled_shapes, (((0,), (0,)), ((), ())), preferred_element_type=f32
    ).astype(bf16)
    coeffs = lax.psum_scatter(partial_coeffs, "cell", scatter_dimension=0, tiled=True)
    partial_new = lax.dot_general(
        coeffs, interp_weights, (((0,), (0,)), ((), ())), preferred_element_type=f32
    )
    new_coeffs = lax.psum(partial_new, "cell").astype(bf16)
    fields = jnp.dot(mode_shapes, new_coeffs, preferred_element_type=f32).astype(bf16)

    partial_gram = (
        lax.dot_general(gathered, weighted, (((0,), (0,)), ((), ())), preferred_element_type=f32)
        / total_cells
    ).astype(bf16)
    gram = lax.psum_scatter(partial_gram, "cell", scatter_dimension=0, tiled=True)
    return (gram.astype(f32), fields)


def pick(step, table, default):
    value = jnp.int32(default)
    for at, entry in table.items():
        value = jnp.where(step == at, jnp.int32(entry), value)
    return value


def kernel(
    C, Z, total, s_in, vrow_in, v_in, scale_in, w_in, gram, fields,
    s, vrow, v, scale, w, sg, sp, prow, vfull, wf, wfo, so, gsend, grecv, rrecv, gfar, ffar, frecv,
    mpart, msend, mout, mnear, mfar, mg, dm, csend, crecv, cown, kb, wq,
    nown, nsend, nrecv, ksend, krecv, kg,
    loc_sem, ps_sem, pr_sem, xs_sem, xr_sem, zs_sem, zr_sem, gs_sem, gr_sem, fs_sem, fr_sem,
    os_sem, or_sem, us_sem, ur_sem, hs_sem, hr_sem, m1s_sem, m1r_sem, m2s_sem, m2r_sem,
    cs_sem, cr_sem, bs_sem, br_sem, ws_sem, wr_sem, ks_sem, kr_sem, ls_sem, lr_sem, es_sem, er_sem, ds_sem, dr_sem, in_sem,
):
    c, z = lax.axis_index("cell"), lax.axis_index("narrow")
    groups = C // 2
    p, k = c // 2, c % 2
    mate = 2 * p + 1 - k
    rows, cols = s.shape
    modes = v.shape[1]
    half = cols // 2
    cw = half // CHUNKS
    mrows = rows // CHUNKS
    hm = modes // 2

    low = z < Z // 2
    out = jnp.where(low, 0, Z - 1)
    inner = jnp.where(low, 1, Z - 2)
    inner2 = Z - 1 - inner
    out2 = Z - 1 - out
    edge = z == out
    mid = z != out
    inward = jnp.where(edge, inner, inner2)

    def remote(src, dst, ssem, rsem, cell, narrow):
        return pltpu.make_async_remote_copy(
            src_ref=src, dst_ref=dst, send_sem=ssem, recv_sem=rsem,
            device_id={"cell": cell, "narrow": narrow}, device_id_type=MESH,
        )

    def rows_chip(h):
        q = pick(h, {0: 0, 1: 3, 2: 1, 3: 2}, 0)
        return jnp.where(low, groups - 1 - q, q)

    def chip(d):
        return (p + d) % groups

    def plane(d):
        return (z + d) % Z

    loads = [
        pltpu.make_async_copy(source, target, in_sem.at[at])
        for at, (source, target) in enumerate(
            ((s_in, s), (v_in, v), (vrow_in, vrow), (w_in, w), (scale_in, scale))
        )
    ]
    for load in loads:
        load.start()

    barrier = pltpu.get_barrier_semaphore()

    def greet(cell, narrow):
        pl.semaphore_signal(
            barrier, inc=1, device_id={"cell": cell, "narrow": narrow}, device_id_type=MESH
        )

    greet(mate, z)
    for d in range(1, groups):
        greet(2 * chip(d) + k, z)
    for d in range(1, Z):
        greet(c, plane(d))
    pl.semaphore_wait(barrier, groups + Z - 1)

    mine = pl.ds(pl.multiple_of(k * rows, rows), rows)
    theirs = pl.ds(pl.multiple_of((1 - k) * rows, rows), rows)

    def local_copy(h):
        lanes = pl.ds(pl.multiple_of(k * half + h * cw, cw), cw)
        return pltpu.make_async_copy(s.at[:, lanes], sg.at[z, h, mine], loc_sem.at[h])

    def mate_copy(h):
        lanes = pl.ds(pl.multiple_of((1 - k) * half + h * cw, cw), cw)
        return remote(s.at[:, lanes], sg.at[z, h, mine], ps_sem.at[h], pr_sem.at[h], mate, z)

    def w_rows(q):
        return pl.ds(pl.multiple_of(q * mrows, mrows), mrows)

    def w_send(q):
        return remote(w.at[w_rows(q)], wq.at[p], ws_sem.at[q], wr_sem.at[p], 2 * q + k, z)

    def w_recv(q):
        return remote(w.at[w_rows(q)], wq.at[q], ws_sem.at[q], wr_sem.at[q], 2 * q + k, z)

    def in_copy(b, h):
        return remote(sg.at[b, h], sg.at[b, h], zs_sem.at[0, b, h], zr_sem.at[b, h], c, inward)

    def out_copy(b, h):
        return remote(sg.at[b, h], sg.at[b, h], zs_sem.at[1, b, h], zr_sem.at[b, h], c, out)

    def m_near(q):
        return remote(msend.at[q], mnear.at[q], m1s_sem.at[q], m1r_sem.at[q], c, inward)

    def m_far(q):
        return remote(msend.at[q], mfar.at[q], m1s_sem.at[q], m2r_sem.at[q], c, inward)

    def m_out(q):
        return remote(mout.at[q], mfar.at[q], m2s_sem.at[q], m2r_sem.at[q], c, out)

    block_copy = remote(s, sp, xs_sem.at[0], xr_sem.at[0], mate, z)
    vol_copy = remote(vrow, prow, xs_sem.at[1], xr_sem.at[1], mate, z)
    new_half = remote(nsend, nrecv, xs_sem.at[2], xr_sem.at[2], mate, z)

    def d_rows(q):
        return pl.ds(pl.multiple_of(k * rows + q * mrows, mrows), mrows)

    def d_copy(q):
        return remote(dm.at[d_rows(q)], dm.at[d_rows(q)], ds_sem.at[q], dr_sem.at[q], mate, z)

    def shape(q, value):
        mg[q * mrows:(q + 1) * mrows, :] = value.astype(BF16)
        dm[d_rows(q), :] = (value * vfull[d_rows(q), :1]).astype(BF16)
        d_copy(q).start()

    loads[0].wait()
    for h in range(CHUNKS):
        local_copy(h).start()
        mate_copy(h).start()
    block_copy.start()
    loads[2].wait()
    vol_copy.start()
    loads[3].wait()
    for d in (1, 2, 3):
        w_send(chip(d)).start()

    loads[1].wait()
    mpart[...] = jnp.dot(s[...], v[...], preferred_element_type=F32).reshape(mpart.shape)

    loads[4].wait()

    @pl.when(edge)
    def _():
        for q in range(CHUNKS):
            msend[q] = mpart[q].astype(BF16)
            m_near(q).start()

    for h in range(CHUNKS):
        local_copy(h).wait()
        mate_copy(h).wait_recv()

        @pl.when(edge)
        def _():
            in_copy(z, h).start()

        if h == 0:
            @pl.when(mid)
            def _():
                in_copy(z, h).start()

        if h < 2:
            @pl.when(mid)
            def _():
                out_copy(z, h).start()

    def column(row):
        return jnp.broadcast_to(row[...], (128, rows)).T

    vfull[mine, :] = column(vrow)
    wf[mine, :] = (s[...].astype(F32) * vfull[mine, :1]).astype(BF16)
    vol_copy.wait_recv()
    vfull[theirs, :] = column(prow)
    block_copy.wait_recv()
    wf[theirs, :] = (sp[...].astype(F32) * vfull[theirs, :1]).astype(BF16)

    def apart(b):
        return jnp.where(p // 2 == b // 2, 0, 2) + jnp.where(p % 2 == b % 2, 0, 1)

    def flip(b, d):
        row = 1 - b // 2 if d == 2 else b // 2
        col = 1 - b % 2 if d == 1 else b % 2
        return 2 * row + col

    def direct(t, h, e, to):
        d = jnp.where(apart(to) == 1, 0, 1)
        r = jnp.where(t == FAR, CHUNKS, h)
        return remote(
            gsend.at[t, h, e], grecv.at[d, r, e], gs_sem.at[t, h, e], gr_sem.at[d, r, e],
            2 * to + k, z,
        )

    def across(t, h, e, to):
        return remote(
            gsend.at[t, h, e], rrecv.at[t, h], fs_sem.at[t, h, e], fr_sem.at[t, h],
            2 * flip(to, 1 if e == 0 else 2) + k, z,
        )

    def term(t, b, h, to, weights):
        value = lax.dot_general(
            sg[b, h], weights[...], (((0,), (0,)), ((), ())), preferred_element_type=F32
        ) * (1.0 / total)
        where = apart(to)

        @pl.when((where == 0) & (t != FAR))
        def _():
            gram[pl.ds(pl.multiple_of(h * cw, cw), cw), :] = value

        @pl.when((where == 0) & (t == FAR))
        def _():
            gfar[...] = value

        @pl.when(where != 0)
        def _():
            for e in range(2):
                gsend[t, h, e] = value[:, e * half:(e + 1) * half].astype(BF16)

        @pl.when(where == 3)
        def _():
            for e in range(2):
                across(t, h, e, to).start()

        @pl.when(where == 1)
        def _():
            direct(t, h, 1, to).start()

        @pl.when(where == 2)
        def _():
            direct(t, h, 0, to).start()

    def relay(t, h, to):
        where = apart(to)
        for e in range(2):
            @pl.when(where == e + 1)
            def _():
                across(t, h, e, to).wait_recv()
                gsend[t, h, e] = (
                    gsend[t, h, e].astype(F32) + rrecv[t, h].astype(F32)
                ).astype(BF16)
                direct(t, h, e, to).start()

    @pl.when(mid)
    def _():
        @pl.loop(0, EARLY)
        def _(h):
            term(z, z, h, z, wf)

    @pl.when(edge)
    def _():
        @pl.loop(0, 2)
        def _(h):
            in_copy(inner, h).wait_recv()
            term(inner, inner, h, inner, wf)

    def near(q):
        m_near(q).wait_recv()
        msend[q] = (mpart[q] + mnear[q].astype(F32)).astype(BF16)
        m_far(q).start()

    def far(q):
        m_out(q).wait_recv()
        value = mpart[q] + mfar[q].astype(F32)
        mout[q] = value.astype(BF16)
        m_out(q).start()
        shape(q, value + mnear[q].astype(F32))

    @pl.when(mid)
    def _():
        near(0)
        near(1)
        near(2)
        far(0)
        near(3)
        in_copy(z, 1).start()
        far(1)
        far(2)
        far(3)
        out_copy(z, 2).start()
        out_copy(z, 3).start()

    @pl.when(edge)
    def _():
        for q in range(CHUNKS):
            m_out(q).wait_recv()
            shape(q, mpart[q] + mfar[q].astype(F32))

    def o_copy(h):
        return remote(sg.at[out, h], so.at[h], os_sem.at[h], or_sem.at[h], mate, z)

    def o_weigh(block, h, core):
        lanes = pl.ds(pl.multiple_of(core * half + h * cw, cw), cw)
        wfo[:, lanes] = (block.astype(F32) * vfull[:, :1]).astype(BF16)

    def k_send(h):
        return remote(csend.at[h], crecv.at[p], cs_sem.at[h], cr_sem.at[p], 2 * h + k, z)

    def k_recv(q):
        return remote(csend.at[q], crecv.at[q], cs_sem.at[q], cr_sem.at[q], 2 * q + k, z)

    def k_share(t, b):
        return remote(kb.at[b], kb.at[b], bs_sem.at[t], br_sem.at[b], c, t)

    def n_send(q):
        return remote(ksend.at[q], krecv.at[p], ks_sem.at[q], kr_sem.at[p], 2 * q + k, z)

    def n_recv(q):
        return remote(ksend.at[q], krecv.at[q], ks_sem.at[q], kr_sem.at[q], 2 * q + k, z)

    def n_share(q, b):
        return remote(kg.at[k, b], kg.at[k, b], ls_sem.at[q], lr_sem.at[b], 2 * q + k, z)

    def n_mate(q, core):
        return remote(kg.at[core, q], kg.at[core, q], es_sem.at[q], er_sem.at[q], mate, z)

    def coefficients():
        for q in range(CHUNKS):
            d_copy(q).wait_recv()

        @pl.loop(0, CHUNKS)
        def _(h):
            value = lax.dot_general(
                sg[z, h], dm[...], (((0,), (0,)), ((), ())), preferred_element_type=F32
            )

            @pl.when(h == p)
            def _():
                cown[...] = value

            @pl.when(h != p)
            def _():
                csend[h] = value.astype(BF16)
                k_send(h).start()

    def coefficient_sum():
        value = cown[...]
        for d in (1, 2, 3):
            q = chip(d)
            k_recv(q).wait_recv()
            value = value + crecv[q].astype(F32)
        kb[z] = (value * (scale[...] * (1.0 / total))).astype(BF16)
        for d in (3, 2, 1):
            k_share(plane(d), z).start()

    def new_part():
        for d in (1, 2, 3):
            w_recv(chip(d)).wait_recv()
            k_share(plane(d), plane(d)).wait_recv()
        wq[p] = w[w_rows(p), :]
        value = lax.dot_general(
            kb[...].reshape(rows, modes), wq[...].reshape(rows, w.shape[1]),
            (((0,), (0,)), ((), ())), preferred_element_type=F32,
        )

        @pl.when(k == 0)
        def _():
            nown[...] = value[:hm]
            nsend[...] = value[hm:]

        @pl.when(k == 1)
        def _():
            nown[...] = value[hm:]
            nsend[...] = value[:hm]

        new_half.start()

    def new_scatter():
        new_half.wait_recv()
        value = nown[...] + nrecv[...]
        nown[...] = value
        ksend[...] = value.astype(BF16).reshape(ksend.shape)
        for d in (3, 1, 2):
            n_send(chip(d)).start()

    def new_sum():
        piece = hm // groups
        value = nown[pl.ds(pl.multiple_of(p * piece, piece), piece), :]
        for d in (1, 2, 3):
            q = chip(d)
            n_recv(q).wait_recv()
            value = value + krecv[q].astype(F32)
        kg[k, p] = value.astype(BF16)
        for d in (3, 1, 2):
            n_share(chip(d), p).start()
        n_mate(p, k).start()

    def new_gather():
        for d in (1, 2, 3):
            q = chip(d)
            n_share(q, q).wait_recv()
            n_mate(q, k).start()

    def reconstruct():
        for q in range(groups):
            n_mate(q, 1 - k).wait_recv()
        fields[...] = jnp.dot(
            mg[...], kg[...].reshape(modes, w.shape[1]), preferred_element_type=F32
        ).astype(BF16)

    own_rows = pick(jnp.where(low, groups - 1 - p, p), {0: 0, 3: 1, 1: 2, 2: 3}, 0)

    def far_send():
        return remote(ffar, frecv.at[own_rows], us_sem.at[0], ur_sem.at[own_rows], c, out)

    def far_share(q):
        return remote(frecv.at[q], frecv.at[q], hs_sem.at[0], ur_sem.at[q], 2 * out2 + k, z)

    def far_sum():
        value = gfar[...]
        for d in range(2):
            for e in range(2):
                to = flip(p, d + 1)
                remote(
                    gsend.at[FAR, 0, e], grecv.at[d, CHUNKS, e], gs_sem.at[FAR, 0, e],
                    gr_sem.at[d, CHUNKS, e], 2 * to + k, z,
                ).wait_recv()
        parts = [
            (grecv[0, CHUNKS, e].astype(F32) + grecv[1, CHUNKS, e].astype(F32)) for e in range(2)
        ]
        ffar[...] = (value + jnp.concatenate(parts, axis=1)).astype(BF16)
        far_send().start()

    OUT2, OUT, IN2, IN, ROWS = range(5)
    mid_terms = {
        0: (IN2, 0), 2: (OUT, 0), 3: (IN2, 1), 4: (OUT, 1), 5: (IN, 2), 6: (OUT2, 0), 7: (OUT, 2),
        8: (IN, 3), 9: (OUT, 3), 10: (OUT2, 1), 11: (ROWS, 0), 12: (ROWS, 1), 13: (OUT2, 2),
        14: (ROWS, 2), 16: (OUT2, 3), 17: (ROWS, 3), 18: (IN2, 2), 19: (IN2, 3),
    }
    mid_relays = {
        0: (IN, 0), 1: (IN, 1), 3: (IN2, 0), 5: (OUT, 0), 6: (IN2, 1), 7: (OUT, 1), 8: (IN, 2),
        10: (OUT2, 0), 11: (OUT, 2), 12: (OUT, 3), 13: (IN, 3), 14: (ROWS, 0), 15: (OUT2, 2),
        18: (ROWS, 2), 19: (ROWS, 3), 21: (IN2, 2),
    }
    mid_more = {13: (OUT2, 1), 14: (ROWS, 1), 19: (OUT2, 3), 21: (IN2, 3)}
    edge_terms = {
        2: (OUT, 0), 3: (OUT, 1), 4: (OUT, 2), 5: (OUT, 3), 6: (IN, 2), 7: (IN, 3), 10: (IN2, 0),
        14: (IN2, 1), 18: (IN2, 2), 20: (IN2, 3),
    }
    edge_relays = {
        2: (IN, 0), 3: (IN, 1), 5: (OUT, 0), 6: (OUT, 1), 7: (OUT, 2), 8: (OUT, 3), 9: (IN, 2),
        10: (IN, 3), 14: (IN2, 0), 16: (IN2, 1), 20: (IN2, 2), 21: (IN2, 3),
    }
    STEPS = 23

    def decode(step, for_mid, for_edge):
        def code(table):
            return {at: 4 * entry[0] + entry[1] for at, entry in table.items()}

        event = jnp.where(edge, pick(step, code(for_edge), -4), pick(step, code(for_mid), -4))
        kind, h = (event + 4) // 4 - 1, (event + 4) % 4
        b = jnp.where(
            kind == OUT, out, jnp.where(kind == IN2, inner2, jnp.where(kind == IN, inner, out2))
        )
        t = jnp.where(kind == ROWS, FAR, b)
        to = jnp.where(kind == ROWS, rows_chip(h), b)
        return kind, h, b, t, to

    def relay_step(step, for_mid, for_edge):
        kind, h, b, t, to = decode(step, for_mid, for_edge)

        @pl.when(kind >= 0)
        def _():
            relay(t, h, to)

    @pl.loop(0, STEPS)
    def _(step):
        kind, h, b, t, to = decode(step, mid_terms, edge_terms)

        @pl.when((kind >= 0) & (kind != ROWS))
        def _():
            @pl.when(b != z)
            def _():
                in_copy(b, h).wait_recv()

            @pl.when(mid & (kind == OUT))
            def _():
                in_copy(b, h).start()
                o_copy(h).start()

            @pl.when(mid & (kind == IN2))
            def _():
                out_copy(b, h).start()

            @pl.when(mid & (kind == OUT) & (h == CHUNKS - 1))
            def _():
                in_copy(z, 2).start()
                in_copy(z, 3).start()

            term(t, b, h, to, wf)

            @pl.when(mid & (kind == OUT))
            def _():
                o_weigh(sg[b, h], h, k)

        @pl.when(mid & (step == 11))
        def _():
            for q in range(CHUNKS):
                o_copy(q).wait_recv()
                o_weigh(so[q], q, 1 - k)

        @pl.when(kind == ROWS)
        def _():
            term(t, b, h, to, wfo)

        @pl.when(step == 1)
        def _():
            coefficients()

        @pl.when(step == 5)
        def _():
            coefficient_sum()

        @pl.when(step == 12)
        def _():
            new_part()

        @pl.when(step == 12)
        def _():
            new_scatter()

        @pl.when(step == 17)
        def _():
            new_sum()

        @pl.when(step == 22)
        def _():
            new_gather()

        relay_step(step, mid_relays, edge_relays)
        relay_step(step, mid_more, {})

        @pl.when(mid & (step == 19 + own_rows // 2))
        def _():
            far_sum()

        @pl.when(edge & (p != out2) & (step == STEPS - 1))
        def _():
            far_send().wait_recv()
            far_share(own_rows).start()

    reconstruct()

    @pl.when(mid | (p != out2))
    def _():
        @pl.loop(0, CHUNKS)
        def _(h):
            at = pl.ds(pl.multiple_of(h * cw, cw), cw)
            for d in range(2):
                to = flip(p, d + 1)
                for e in range(2):
                    remote(
                        gsend.at[p, h, e], grecv.at[d, h, e], gs_sem.at[p, h, e],
                        gr_sem.at[d, h, e], 2 * to + k, z,
                    ).wait_recv()
            for e in range(2):
                lanes = slice(e * half, (e + 1) * half)
                gram[at, lanes] = (
                    gram[at, lanes] + grecv[0, h, e].astype(F32) + grecv[1, h, e].astype(F32)
                )

    @pl.when(edge & (p == out2))
    def _():
        @pl.loop(0, CHUNKS)
        def _(h):
            remote(
                frecv.at[h], frecv.at[h], hs_sem.at[0], ur_sem.at[h], mate, z
            ).wait_recv()
            gram[pl.ds(pl.multiple_of(h * cw, cw), cw), :] = frecv[h].astype(F32)

    vol_copy.wait_send()
    block_copy.wait_send()
    new_half.wait_send()
    for h in range(CHUNKS):
        mate_copy(h).wait_send()
        m_near(h).wait_send()
        n_mate(h, k).wait_send()
        d_copy(h).wait_send()

        @pl.when(h != p)
        def _():
            k_send(h).wait_send()
    for d in (1, 2, 3):
        w_send(chip(d)).wait_send()
        n_send(chip(d)).wait_send()
        n_share(chip(d), p).wait_send()
        k_share(plane(d), z).wait_send()

    @pl.when(edge & (p != out2))
    def _():
        far_share(own_rows).wait_send()

    def sent(t, h, to):
        where = apart(to)

        @pl.when((where == 1) | (where == 2))
        def _():
            for e in range(2):
                direct(t, h, e, to).wait_send()

        @pl.when(where == 3)
        def _():
            for e in range(2):
                across(t, h, e, to).wait_send()

    @pl.loop(0, CHUNKS)
    def _(h):
        in_copy(z, h).wait_send()
        for b in range(Z):
            @pl.when(mid | (b != out2))
            def _():
                sent(b, h, b)

        @pl.when(mid)
        def _():
            in_copy(out, h).wait_send()
            out_copy(z, h).wait_send()
            out_copy(inner2, h).wait_send()
            m_out(h).wait_send()
            o_copy(h).wait_send()
            sent(FAR, h, rows_chip(h))

    @pl.when(mid)
    def _():
        far_send().wait_send()


def shards_kernel(snapshots, cell_volume, mode_vectors, mode_scale, interp_weights):
    C, Z = lax.axis_size("cell"), lax.axis_size("narrow")
    groups = C // 2
    rows, cols = snapshots.shape
    modes = mode_vectors.shape[1]
    conds = interp_weights.shape[1]
    half = cols // 2
    cw = half // CHUNKS
    mrows = rows // CHUNKS
    hm = modes // 2
    dma = pltpu.SemaphoreType.DMA
    vmem = pl.BlockSpec(memory_space=pltpu.VMEM)
    inputs = (snapshots, cell_volume[None, :], mode_vectors, mode_scale[None, :], interp_weights)
    inputs = [pltpu.with_memory_space_constraint(x, pltpu.HBM) for x in inputs]
    return pl.pallas_call(
        functools.partial(kernel, C, Z, rows * C),
        out_shape=(
            jax.ShapeDtypeStruct((half, cols), F32),
            jax.ShapeDtypeStruct((rows, conds), BF16),
        ),
        in_specs=[pl.BlockSpec(memory_space=pltpu.HBM)] * 5,
        out_specs=(vmem, vmem),
        scratch_shapes=[
            pltpu.VMEM((rows, cols), BF16),
            pltpu.VMEM((1, rows), F32),
            pltpu.VMEM((cols, modes), BF16),
            pltpu.VMEM((1, modes), F32),
            pltpu.VMEM((rows, conds), BF16),
            pltpu.VMEM((Z, CHUNKS, 2 * rows, cw), BF16),
            pltpu.VMEM((rows, cols), BF16),
            pltpu.VMEM((1, rows), F32),
            pltpu.VMEM((2 * rows, 128), F32),
            pltpu.VMEM((2 * rows, cols), BF16),
            pltpu.VMEM((2 * rows, cols), BF16),
            pltpu.VMEM((CHUNKS, 2 * rows, cw), BF16),
            pltpu.VMEM((FAR + 1, CHUNKS, 2, cw, half), BF16),
            pltpu.VMEM((2, CHUNKS + 1, 2, cw, half), BF16),
            pltpu.VMEM((FAR + 1, CHUNKS, cw, half), BF16),
            pltpu.VMEM((cw, cols), F32),
            pltpu.VMEM((cw, cols), BF16),
            pltpu.VMEM((CHUNKS, cw, cols), BF16),
            pltpu.VMEM((CHUNKS, mrows, modes), F32),
            pltpu.VMEM((CHUNKS, mrows, modes), BF16),
            pltpu.VMEM((CHUNKS, mrows, modes), BF16),
            pltpu.VMEM((CHUNKS, mrows, modes), BF16),
            pltpu.VMEM((CHUNKS, mrows, modes), BF16),
            pltpu.VMEM((rows, modes), BF16),
            pltpu.VMEM((2 * rows, modes), BF16),
            pltpu.VMEM((CHUNKS, cw, modes), BF16),
            pltpu.VMEM((CHUNKS, cw, modes), BF16),
            pltpu.VMEM((cw, modes), F32),
            pltpu.VMEM((Z, cw, modes), BF16),
            pltpu.VMEM((groups, mrows, conds), BF16),
            pltpu.VMEM((hm, conds), F32),
            pltpu.VMEM((hm, conds), F32),
            pltpu.VMEM((hm, conds), F32),
            pltpu.VMEM((groups, hm // groups, conds), BF16),
            pltpu.VMEM((groups, hm // groups, conds), BF16),
            pltpu.VMEM((2, groups, hm // groups, conds), BF16),
            dma((CHUNKS,)), dma((CHUNKS,)), dma((CHUNKS,)),
            dma((3,)), dma((3,)),
            dma((2, Z, CHUNKS)), dma((Z, CHUNKS)),
            dma((FAR + 1, CHUNKS, 2)), dma((2, CHUNKS + 1, 2)),
            dma((FAR + 1, CHUNKS, 2)), dma((FAR + 1, CHUNKS)),
            dma((CHUNKS,)), dma((CHUNKS,)),
            dma((1,)), dma((CHUNKS,)), dma((1,)), dma((1,)),
            dma((CHUNKS,)), dma((CHUNKS,)), dma((CHUNKS,)), dma((CHUNKS,)),
            dma((CHUNKS,)), dma((CHUNKS,)), dma((Z,)), dma((Z,)),
            dma((groups,)), dma((groups,)), dma((groups,)), dma((groups,)),
            dma((groups,)), dma((groups,)), dma((groups,)), dma((groups,)),
            dma((CHUNKS,)), dma((CHUNKS,)), dma((5,)),
        ],
        compiler_params=pltpu.CompilerParams(
            collective_id=0, has_side_effects=True, vmem_limit_bytes=45 * 1024 * 1024
        ),
    )(*inputs)


def shards(snapshots, cell_volume, mode_vectors, mode_scale, interp_weights):
    C, Z = lax.axis_size("cell"), lax.axis_size("narrow")
    rows, cols = snapshots.shape
    modes = mode_vectors.shape[1]
    fits = (
        C == 2 * Z == 8
        and C == 2 * CHUNKS
        and cols % (2 * 128 * CHUNKS) == 0
        and rows % (16 * Z) == 0
        and modes % (16 * C) == 0
        and interp_weights.shape[0] == rows == cols // 2
        and rows * cols <= 512 * 1024
        and interp_weights.shape[1] <= 1024
        and modes <= 512
    )
    run = shards_kernel if fits else shards_xla
    return run(snapshots, cell_volume, mode_vectors, mode_scale, interp_weights)


def solution(mesh):
    return jax.shard_map(
        shards,
        mesh=mesh,
        in_specs=(P("cell", "narrow"), P("cell"), P("narrow", None), P(), P("cell", "narrow")),
        out_specs=(P("cell", "narrow"), P("cell", "narrow")),
        check_vma=False,
    )
```

```python
import functools

import jax
import jax.numpy as jnp
from jax import lax
from jax.experimental import pallas as pl
from jax.experimental.pallas import tpu as pltpu
from jax.sharding import PartitionSpec as P

F32, BF16 = jnp.float32, jnp.bfloat16
MESH = pl.DeviceIdType.MESH
CHUNKS = 4
FAR = 4
EARLY = 2


def shards_xla(snapshots, cell_volume, mode_vectors, mode_scale, interp_weights):
    f32, bf16 = jnp.float32, jnp.bfloat16
    n_cell, n_narrow = lax.axis_size("cell"), lax.axis_size("narrow")
    total_cells = snapshots.shape[0] * n_cell
    rows = interp_weights.shape[0]
    weighted = (snapshots.astype(f32) * cell_volume[:, None]).astype(bf16)

    partial_shapes = jnp.dot(snapshots, mode_vectors, preferred_element_type=f32)
    mode_shapes = lax.psum(partial_shapes, "narrow").astype(bf16)

    gathered = lax.all_gather(snapshots, "narrow", axis=1, tiled=True)
    scaled_shapes = (
        mode_shapes.astype(f32) * (cell_volume / total_cells)[:, None] * mode_scale[None, :]
    ).astype(bf16)
    partial_coeffs = lax.dot_general(
        gathered, scaled_shapes, (((0,), (0,)), ((), ())), preferred_element_type=f32
    ).astype(bf16)
    coeffs = lax.psum_scatter(partial_coeffs, "cell", scatter_dimension=0, tiled=True)
    partial_new = lax.dot_general(
        coeffs, interp_weights, (((0,), (0,)), ((), ())), preferred_element_type=f32
    )
    new_coeffs = lax.psum(partial_new, "cell").astype(bf16)
    fields = jnp.dot(mode_shapes, new_coeffs, preferred_element_type=f32).astype(bf16)

    partial_gram = (
        lax.dot_general(gathered, weighted, (((0,), (0,)), ((), ())), preferred_element_type=f32)
        / total_cells
    ).astype(bf16)
    gram = lax.psum_scatter(partial_gram, "cell", scatter_dimension=0, tiled=True)
    return (gram.astype(f32), fields)


def pick(step, table, default):
    value = jnp.int32(default)
    for at, entry in table.items():
        value = jnp.where(step == at, jnp.int32(entry), value)
    return value


def kernel(
    C, Z, total, s_in, vrow_in, v_in, scale_in, w_in, gram, fields,
    s, vrow, v, scale, w, sg, sp, prow, vfull, wf, wfo, so, gsend, grecv, rrecv, gfar, ffar, frecv,
    mpart, msend, mout, mnear, mfar, mg, dm, csend, crecv, cown, kb, wq,
    nown, nsend, nrecv, ksend, krecv, kg,
    loc_sem, ps_sem, pr_sem, xs_sem, xr_sem, zs_sem, zr_sem, gs_sem, gr_sem, fs_sem, fr_sem,
    os_sem, or_sem, us_sem, ur_sem, hs_sem, hr_sem, m1s_sem, m1r_sem, m2s_sem, m2r_sem,
    cs_sem, cr_sem, bs_sem, br_sem, ws_sem, wr_sem, ks_sem, kr_sem, ls_sem, lr_sem, es_sem, er_sem, ds_sem, dr_sem, in_sem,
):
    c, z = lax.axis_index("cell"), lax.axis_index("narrow")
    groups = C // 2
    p, k = c // 2, c % 2
    mate = 2 * p + 1 - k
    rows, cols = s.shape
    modes = v.shape[1]
    half = cols // 2
    cw = half // CHUNKS
    mrows = rows // CHUNKS
    hm = modes // 2

    low = z < Z // 2
    out = jnp.where(low, 0, Z - 1)
    inner = jnp.where(low, 1, Z - 2)
    inner2 = Z - 1 - inner
    out2 = Z - 1 - out
    edge = z == out
    mid = z != out
    inward = jnp.where(edge, inner, inner2)

    def remote(src, dst, ssem, rsem, cell, narrow):
        return pltpu.make_async_remote_copy(
            src_ref=src, dst_ref=dst, send_sem=ssem, recv_sem=rsem,
            device_id={"cell": cell, "narrow": narrow}, device_id_type=MESH,
        )

    def rows_chip(h):
        q = pick(h, {0: 0, 1: 3, 2: 1, 3: 2}, 0)
        return jnp.where(low, groups - 1 - q, q)

    def chip(d):
        return (p + d) % groups

    def plane(d):
        return (z + d) % Z

    loads = [
        pltpu.make_async_copy(source, target, in_sem.at[at])
        for at, (source, target) in enumerate(
            ((s_in, s), (v_in, v), (vrow_in, vrow), (w_in, w), (scale_in, scale))
        )
    ]
    for load in loads:
        load.start()

    barrier = pltpu.get_barrier_semaphore()

    def greet(cell, narrow):
        pl.semaphore_signal(
            barrier, inc=1, device_id={"cell": cell, "narrow": narrow}, device_id_type=MESH
        )

    greet(mate, z)
    for d in range(1, groups):
        greet(2 * chip(d) + k, z)
    for d in range(1, Z):
        greet(c, plane(d))
    pl.semaphore_wait(barrier, groups + Z - 1)

    mine = pl.ds(pl.multiple_of(k * rows, rows), rows)
    theirs = pl.ds(pl.multiple_of((1 - k) * rows, rows), rows)

    def local_copy(h):
        lanes = pl.ds(pl.multiple_of(k * half + h * cw, cw), cw)
        return pltpu.make_async_copy(s.at[:, lanes], sg.at[z, h, mine], loc_sem.at[h])

    def mate_copy(h):
        lanes = pl.ds(pl.multiple_of((1 - k) * half + h * cw, cw), cw)
        return remote(s.at[:, lanes], sg.at[z, h, mine], ps_sem.at[h], pr_sem.at[h], mate, z)

    def w_rows(q):
        return pl.ds(pl.multiple_of(q * mrows, mrows), mrows)

    def w_send(q):
        return remote(w.at[w_rows(q)], wq.at[p], ws_sem.at[q], wr_sem.at[p], 2 * q + k, z)

    def w_recv(q):
        return remote(w.at[w_rows(q)], wq.at[q], ws_sem.at[q], wr_sem.at[q], 2 * q + k, z)

    def in_copy(b, h):
        return remote(sg.at[b, h], sg.at[b, h], zs_sem.at[0, b, h], zr_sem.at[b, h], c, inward)

    def out_copy(b, h):
        return remote(sg.at[b, h], sg.at[b, h], zs_sem.at[1, b, h], zr_sem.at[b, h], c, out)

    def m_near(q):
        return remote(msend.at[q], mnear.at[q], m1s_sem.at[q], m1r_sem.at[q], c, inward)

    def m_far(q):
        return remote(msend.at[q], mfar.at[q], m1s_sem.at[q], m2r_sem.at[q], c, inward)

    def m_out(q):
        return remote(mout.at[q], mfar.at[q], m2s_sem.at[q], m2r_sem.at[q], c, out)

    block_copy = remote(s, sp, xs_sem.at[0], xr_sem.at[0], mate, z)
    vol_copy = remote(vrow, prow, xs_sem.at[1], xr_sem.at[1], mate, z)
    new_half = remote(nsend, nrecv, xs_sem.at[2], xr_sem.at[2], mate, z)

    def d_rows(q):
        return pl.ds(pl.multiple_of(k * rows + q * mrows, mrows), mrows)

    def d_copy(q):
        return remote(dm.at[d_rows(q)], dm.at[d_rows(q)], ds_sem.at[q], dr_sem.at[q], mate, z)

    def shape(q, value):
        mg[q * mrows:(q + 1) * mrows, :] = value.astype(BF16)
        dm[d_rows(q), :] = (value * vfull[d_rows(q), :1]).astype(BF16)
        d_copy(q).start()

    loads[0].wait()
    for h in range(CHUNKS):
        local_copy(h).start()
        mate_copy(h).start()
    block_copy.start()

    loads[1].wait()
    mpart[...] = jnp.dot(s[...], v[...], preferred_element_type=F32).reshape(mpart.shape)

    @pl.when(edge)
    def _():
        for q in range(CHUNKS):
            msend[q] = mpart[q].astype(BF16)
            m_near(q).start()

    for h in range(CHUNKS):
        local_copy(h).wait()
        mate_copy(h).wait_recv()

        @pl.when(edge)
        def _():
            in_copy(z, h).start()

        if h == 0:
            @pl.when(mid)
            def _():
                in_copy(z, h).start()

        if h < 2:
            @pl.when(mid)
            def _():
                out_copy(z, h).start()

    loads[2].wait()
    vol_copy.start()
    loads[3].wait()
    for d in (1, 2, 3):
        w_send(chip(d)).start()
    loads[4].wait()

    def column(row):
        return jnp.broadcast_to(row[...], (128, rows)).T

    vfull[mine, :] = column(vrow)
    wf[mine, :] = (s[...].astype(F32) * vfull[mine, :1]).astype(BF16)
    vol_copy.wait_recv()
    vfull[theirs, :] = column(prow)
    block_copy.wait_recv()
    wf[theirs, :] = (sp[...].astype(F32) * vfull[theirs, :1]).astype(BF16)

    def apart(b):
        return jnp.where(p // 2 == b // 2, 0, 2) + jnp.where(p % 2 == b % 2, 0, 1)

    def flip(b, d):
        row = 1 - b // 2 if d == 2 else b // 2
        col = 1 - b % 2 if d == 1 else b % 2
        return 2 * row + col

    def direct(t, h, e, to):
        d = jnp.where(apart(to) == 1, 0, 1)
        r = jnp.where(t == FAR, CHUNKS, h)
        return remote(
            gsend.at[t, h, e], grecv.at[d, r, e], gs_sem.at[t, h, e], gr_sem.at[d, r, e],
            2 * to + k, z,
        )

    def across(t, h, e, to):
        return remote(
            gsend.at[t, h, e], rrecv.at[t, h], fs_sem.at[t, h, e], fr_sem.at[t, h],
            2 * flip(to, 1 if e == 0 else 2) + k, z,
        )

    def term(t, b, h, to, weights):
        value = lax.dot_general(
            sg[b, h], weights[...], (((0,), (0,)), ((), ())), preferred_element_type=F32
        ) * (1.0 / total)
        where = apart(to)

        @pl.when((where == 0) & (t != FAR))
        def _():
            gram[pl.ds(pl.multiple_of(h * cw, cw), cw), :] = value

        @pl.when((where == 0) & (t == FAR))
        def _():
            gfar[...] = value

        @pl.when(where != 0)
        def _():
            for e in range(2):
                gsend[t, h, e] = value[:, e * half:(e + 1) * half].astype(BF16)

        @pl.when(where == 3)
        def _():
            for e in range(2):
                across(t, h, e, to).start()

        @pl.when(where == 1)
        def _():
            direct(t, h, 1, to).start()

        @pl.when(where == 2)
        def _():
            direct(t, h, 0, to).start()

    def relay(t, h, to):
        where = apart(to)
        for e in range(2):
            @pl.when(where == e + 1)
            def _():
                across(t, h, e, to).wait_recv()
                gsend[t, h, e] = (
                    gsend[t, h, e].astype(F32) + rrecv[t, h].astype(F32)
                ).astype(BF16)
                direct(t, h, e, to).start()

    @pl.when(mid)
    def _():
        @pl.loop(0, EARLY)
        def _(h):
            term(z, z, h, z, wf)

    @pl.when(edge)
    def _():
        @pl.loop(0, 2)
        def _(h):
            in_copy(inner, h).wait_recv()
            term(inner, inner, h, inner, wf)

    def near(q):
        m_near(q).wait_recv()
        msend[q] = (mpart[q] + mnear[q].astype(F32)).astype(BF16)
        m_far(q).start()

    def far(q):
        m_out(q).wait_recv()
        value = mpart[q] + mfar[q].astype(F32)
        mout[q] = value.astype(BF16)
        m_out(q).start()
        shape(q, value + mnear[q].astype(F32))

    @pl.when(mid)
    def _():
        near(0)
        near(1)
        near(2)
        far(0)
        near(3)
        in_copy(z, 1).start()
        far(1)
        far(2)
        far(3)
        out_copy(z, 2).start()
        out_copy(z, 3).start()

    @pl.when(edge)
    def _():
        for q in range(CHUNKS):
            m_out(q).wait_recv()
            shape(q, mpart[q] + mfar[q].astype(F32))

    def o_copy(h):
        return remote(sg.at[out, h], so.at[h], os_sem.at[h], or_sem.at[h], mate, z)

    def o_weigh(block, h, core):
        lanes = pl.ds(pl.multiple_of(core * half + h * cw, cw), cw)
        wfo[:, lanes] = (block.astype(F32) * vfull[:, :1]).astype(BF16)

    def k_send(h):
        return remote(csend.at[h], crecv.at[p], cs_sem.at[h], cr_sem.at[p], 2 * h + k, z)

    def k_recv(q):
        return remote(csend.at[q], crecv.at[q], cs_sem.at[q], cr_sem.at[q], 2 * q + k, z)

    def k_share(t, b):
        return remote(kb.at[b], kb.at[b], bs_sem.at[t], br_sem.at[b], c, t)

    def n_send(q):
        return remote(ksend.at[q], krecv.at[p], ks_sem.at[q], kr_sem.at[p], 2 * q + k, z)

    def n_recv(q):
        return remote(ksend.at[q], krecv.at[q], ks_sem.at[q], kr_sem.at[q], 2 * q + k, z)

    def n_share(q, b):
        return remote(kg.at[k, b], kg.at[k, b], ls_sem.at[q], lr_sem.at[b], 2 * q + k, z)

    def n_mate(q, core):
        return remote(kg.at[core, q], kg.at[core, q], es_sem.at[q], er_sem.at[q], mate, z)

    def coefficients():
        for q in range(CHUNKS):
            d_copy(q).wait_recv()

        @pl.loop(0, CHUNKS)
        def _(h):
            value = lax.dot_general(
                sg[z, h], dm[...], (((0,), (0,)), ((), ())), preferred_element_type=F32
            )

            @pl.when(h == p)
            def _():
                cown[...] = value

            @pl.when(h != p)
            def _():
                csend[h] = value.astype(BF16)
                k_send(h).start()

    def coefficient_sum():
        value = cown[...]
        for d in (1, 2, 3):
            q = chip(d)
            k_recv(q).wait_recv()
            value = value + crecv[q].astype(F32)
        kb[z] = (value * (scale[...] * (1.0 / total))).astype(BF16)
        for d in (3, 2, 1):
            k_share(plane(d), z).start()

    def new_part():
        for d in (1, 2, 3):
            w_recv(chip(d)).wait_recv()
            k_share(plane(d), plane(d)).wait_recv()
        wq[p] = w[w_rows(p), :]
        value = lax.dot_general(
            kb[...].reshape(rows, modes), wq[...].reshape(rows, w.shape[1]),
            (((0,), (0,)), ((), ())), preferred_element_type=F32,
        )

        @pl.when(k == 0)
        def _():
            nown[...] = value[:hm]
            nsend[...] = value[hm:]

        @pl.when(k == 1)
        def _():
            nown[...] = value[hm:]
            nsend[...] = value[:hm]

        new_half.start()

    def new_scatter():
        new_half.wait_recv()
        value = nown[...] + nrecv[...]
        nown[...] = value
        ksend[...] = value.astype(BF16).reshape(ksend.shape)
        for d in (3, 1, 2):
            n_send(chip(d)).start()

    def new_sum():
        piece = hm // groups
        value = nown[pl.ds(pl.multiple_of(p * piece, piece), piece), :]
        for d in (1, 2, 3):
            q = chip(d)
            n_recv(q).wait_recv()
            value = value + krecv[q].astype(F32)
        kg[k, p] = value.astype(BF16)
        for d in (3, 1, 2):
            n_share(chip(d), p).start()
        n_mate(p, k).start()

    def new_gather():
        for d in (1, 2, 3):
            q = chip(d)
            n_share(q, q).wait_recv()
            n_mate(q, k).start()

    def reconstruct():
        for q in range(groups):
            n_mate(q, 1 - k).wait_recv()
        fields[...] = jnp.dot(
            mg[...], kg[...].reshape(modes, w.shape[1]), preferred_element_type=F32
        ).astype(BF16)

    own_rows = pick(jnp.where(low, groups - 1 - p, p), {0: 0, 3: 1, 1: 2, 2: 3}, 0)

    def far_send():
        return remote(ffar, frecv.at[own_rows], us_sem.at[0], ur_sem.at[own_rows], c, out)

    def far_share(q):
        return remote(frecv.at[q], frecv.at[q], hs_sem.at[0], ur_sem.at[q], 2 * out2 + k, z)

    def far_sum():
        value = gfar[...]
        for d in range(2):
            for e in range(2):
                to = flip(p, d + 1)
                remote(
                    gsend.at[FAR, 0, e], grecv.at[d, CHUNKS, e], gs_sem.at[FAR, 0, e],
                    gr_sem.at[d, CHUNKS, e], 2 * to + k, z,
                ).wait_recv()
        parts = [
            (grecv[0, CHUNKS, e].astype(F32) + grecv[1, CHUNKS, e].astype(F32)) for e in range(2)
        ]
        ffar[...] = (value + jnp.concatenate(parts, axis=1)).astype(BF16)
        far_send().start()

    OUT2, OUT, IN2, IN, ROWS = range(5)
    mid_terms = {
        0: (IN2, 0), 2: (OUT, 0), 3: (IN2, 1), 4: (OUT, 1), 5: (IN, 2), 6: (OUT2, 0), 7: (OUT, 2),
        8: (IN, 3), 9: (OUT, 3), 10: (OUT2, 1), 11: (ROWS, 0), 12: (ROWS, 1), 13: (OUT2, 2),
        14: (ROWS, 2), 16: (OUT2, 3), 17: (ROWS, 3), 18: (IN2, 2), 19: (IN2, 3),
    }
    mid_relays = {
        0: (IN, 0), 1: (IN, 1), 3: (IN2, 0), 5: (OUT, 0), 6: (IN2, 1), 7: (OUT, 1), 8: (IN, 2),
        10: (OUT2, 0), 11: (OUT, 2), 12: (OUT, 3), 13: (IN, 3), 14: (ROWS, 0), 15: (OUT2, 2),
        18: (ROWS, 2), 19: (ROWS, 3), 21: (IN2, 2),
    }
    mid_more = {13: (OUT2, 1), 14: (ROWS, 1), 19: (OUT2, 3), 21: (IN2, 3)}
    edge_terms = {
        2: (OUT, 0), 3: (OUT, 1), 4: (OUT, 2), 5: (OUT, 3), 6: (IN, 2), 7: (IN, 3), 10: (IN2, 0),
        14: (IN2, 1), 18: (IN2, 2), 20: (IN2, 3),
    }
    edge_relays = {
        2: (IN, 0), 3: (IN, 1), 5: (OUT, 0), 6: (OUT, 1), 7: (OUT, 2), 8: (OUT, 3), 9: (IN, 2),
        10: (IN, 3), 14: (IN2, 0), 16: (IN2, 1), 20: (IN2, 2), 21: (IN2, 3),
    }
    STEPS = 23

    def decode(step, for_mid, for_edge):
        def code(table):
            return {at: 4 * entry[0] + entry[1] for at, entry in table.items()}

        event = jnp.where(edge, pick(step, code(for_edge), -4), pick(step, code(for_mid), -4))
        kind, h = (event + 4) // 4 - 1, (event + 4) % 4
        b = jnp.where(
            kind == OUT, out, jnp.where(kind == IN2, inner2, jnp.where(kind == IN, inner, out2))
        )
        t = jnp.where(kind == ROWS, FAR, b)
        to = jnp.where(kind == ROWS, rows_chip(h), b)
        return kind, h, b, t, to

    def relay_step(step, for_mid, for_edge):
        kind, h, b, t, to = decode(step, for_mid, for_edge)

        @pl.when(kind >= 0)
        def _():
            relay(t, h, to)

    @pl.loop(0, STEPS)
    def _(step):
        kind, h, b, t, to = decode(step, mid_terms, edge_terms)

        @pl.when((kind >= 0) & (kind != ROWS))
        def _():
            @pl.when(b != z)
            def _():
                in_copy(b, h).wait_recv()

            @pl.when(mid & (kind == OUT))
            def _():
                in_copy(b, h).start()
                o_copy(h).start()

            @pl.when(mid & (kind == IN2))
            def _():
                out_copy(b, h).start()

            @pl.when(mid & (kind == OUT) & (h == CHUNKS - 1))
            def _():
                in_copy(z, 2).start()
                in_copy(z, 3).start()

            term(t, b, h, to, wf)

            @pl.when(mid & (kind == OUT))
            def _():
                o_weigh(sg[b, h], h, k)

        @pl.when(mid & (step == 11))
        def _():
            for q in range(CHUNKS):
                o_copy(q).wait_recv()
                o_weigh(so[q], q, 1 - k)

        @pl.when(kind == ROWS)
        def _():
            term(t, b, h, to, wfo)

        @pl.when(step == 1)
        def _():
            coefficients()

        @pl.when(step == 5)
        def _():
            coefficient_sum()

        @pl.when(step == 12)
        def _():
            new_part()

        @pl.when(step == 12)
        def _():
            new_scatter()

        @pl.when(step == 17)
        def _():
            new_sum()

        @pl.when(step == 22)
        def _():
            new_gather()

        relay_step(step, mid_relays, edge_relays)
        relay_step(step, mid_more, {})

        @pl.when(mid & (step == 19 + own_rows // 2))
        def _():
            far_sum()

        @pl.when(edge & (p != out2) & (step == STEPS - 1))
        def _():
            far_send().wait_recv()
            far_share(own_rows).start()

    reconstruct()

    @pl.when(mid | (p != out2))
    def _():
        @pl.loop(0, CHUNKS)
        def _(h):
            at = pl.ds(pl.multiple_of(h * cw, cw), cw)
            for d in range(2):
                to = flip(p, d + 1)
                for e in range(2):
                    remote(
                        gsend.at[p, h, e], grecv.at[d, h, e], gs_sem.at[p, h, e],
                        gr_sem.at[d, h, e], 2 * to + k, z,
                    ).wait_recv()
            for e in range(2):
                lanes = slice(e * half, (e + 1) * half)
                gram[at, lanes] = (
                    gram[at, lanes] + grecv[0, h, e].astype(F32) + grecv[1, h, e].astype(F32)
                )

    @pl.when(edge & (p == out2))
    def _():
        @pl.loop(0, CHUNKS)
        def _(h):
            remote(
                frecv.at[h], frecv.at[h], hs_sem.at[0], ur_sem.at[h], mate, z
            ).wait_recv()
            gram[pl.ds(pl.multiple_of(h * cw, cw), cw), :] = frecv[h].astype(F32)

    vol_copy.wait_send()
    block_copy.wait_send()
    new_half.wait_send()
    for h in range(CHUNKS):
        mate_copy(h).wait_send()
        m_near(h).wait_send()
        n_mate(h, k).wait_send()
        d_copy(h).wait_send()

        @pl.when(h != p)
        def _():
            k_send(h).wait_send()
    for d in (1, 2, 3):
        w_send(chip(d)).wait_send()
        n_send(chip(d)).wait_send()
        n_share(chip(d), p).wait_send()
        k_share(plane(d), z).wait_send()

    @pl.when(edge & (p != out2))
    def _():
        far_share(own_rows).wait_send()

    def sent(t, h, to):
        where = apart(to)

        @pl.when((where == 1) | (where == 2))
        def _():
            for e in range(2):
                direct(t, h, e, to).wait_send()

        @pl.when(where == 3)
        def _():
            for e in range(2):
                across(t, h, e, to).wait_send()

    @pl.loop(0, CHUNKS)
    def _(h):
        in_copy(z, h).wait_send()
        for b in range(Z):
            @pl.when(mid | (b != out2))
            def _():
                sent(b, h, b)

        @pl.when(mid)
        def _():
            in_copy(out, h).wait_send()
            out_copy(z, h).wait_send()
            out_copy(inner2, h).wait_send()
            m_out(h).wait_send()
            o_copy(h).wait_send()
            sent(FAR, h, rows_chip(h))

    @pl.when(mid)
    def _():
        far_send().wait_send()


def shards_kernel(snapshots, cell_volume, mode_vectors, mode_scale, interp_weights):
    C, Z = lax.axis_size("cell"), lax.axis_size("narrow")
    groups = C // 2
    rows, cols = snapshots.shape
    modes = mode_vectors.shape[1]
    conds = interp_weights.shape[1]
    half = cols // 2
    cw = half // CHUNKS
    mrows = rows // CHUNKS
    hm = modes // 2
    dma = pltpu.SemaphoreType.DMA
    vmem = pl.BlockSpec(memory_space=pltpu.VMEM)
    inputs = (snapshots, cell_volume[None, :], mode_vectors, mode_scale[None, :], interp_weights)
    inputs = [pltpu.with_memory_space_constraint(x, pltpu.HBM) for x in inputs]
    return pl.pallas_call(
        functools.partial(kernel, C, Z, rows * C),
        out_shape=(
            jax.ShapeDtypeStruct((half, cols), F32),
            jax.ShapeDtypeStruct((rows, conds), BF16),
        ),
        in_specs=[pl.BlockSpec(memory_space=pltpu.HBM)] * 5,
        out_specs=(vmem, vmem),
        scratch_shapes=[
            pltpu.VMEM((rows, cols), BF16),
            pltpu.VMEM((1, rows), F32),
            pltpu.VMEM((cols, modes), BF16),
            pltpu.VMEM((1, modes), F32),
            pltpu.VMEM((rows, conds), BF16),
            pltpu.VMEM((Z, CHUNKS, 2 * rows, cw), BF16),
            pltpu.VMEM((rows, cols), BF16),
            pltpu.VMEM((1, rows), F32),
            pltpu.VMEM((2 * rows, 128), F32),
            pltpu.VMEM((2 * rows, cols), BF16),
            pltpu.VMEM((2 * rows, cols), BF16),
            pltpu.VMEM((CHUNKS, 2 * rows, cw), BF16),
            pltpu.VMEM((FAR + 1, CHUNKS, 2, cw, half), BF16),
            pltpu.VMEM((2, CHUNKS + 1, 2, cw, half), BF16),
            pltpu.VMEM((FAR + 1, CHUNKS, cw, half), BF16),
            pltpu.VMEM((cw, cols), F32),
            pltpu.VMEM((cw, cols), BF16),
            pltpu.VMEM((CHUNKS, cw, cols), BF16),
            pltpu.VMEM((CHUNKS, mrows, modes), F32),
            pltpu.VMEM((CHUNKS, mrows, modes), BF16),
            pltpu.VMEM((CHUNKS, mrows, modes), BF16),
            pltpu.VMEM((CHUNKS, mrows, modes), BF16),
            pltpu.VMEM((CHUNKS, mrows, modes), BF16),
            pltpu.VMEM((rows, modes), BF16),
            pltpu.VMEM((2 * rows, modes), BF16),
            pltpu.VMEM((CHUNKS, cw, modes), BF16),
            pltpu.VMEM((CHUNKS, cw, modes), BF16),
            pltpu.VMEM((cw, modes), F32),
            pltpu.VMEM((Z, cw, modes), BF16),
            pltpu.VMEM((groups, mrows, conds), BF16),
            pltpu.VMEM((hm, conds), F32),
            pltpu.VMEM((hm, conds), F32),
            pltpu.VMEM((hm, conds), F32),
            pltpu.VMEM((groups, hm // groups, conds), BF16),
            pltpu.VMEM((groups, hm // groups, conds), BF16),
            pltpu.VMEM((2, groups, hm // groups, conds), BF16),
            dma((CHUNKS,)), dma((CHUNKS,)), dma((CHUNKS,)),
            dma((3,)), dma((3,)),
            dma((2, Z, CHUNKS)), dma((Z, CHUNKS)),
            dma((FAR + 1, CHUNKS, 2)), dma((2, CHUNKS + 1, 2)),
            dma((FAR + 1, CHUNKS, 2)), dma((FAR + 1, CHUNKS)),
            dma((CHUNKS,)), dma((CHUNKS,)),
            dma((1,)), dma((CHUNKS,)), dma((1,)), dma((1,)),
            dma((CHUNKS,)), dma((CHUNKS,)), dma((CHUNKS,)), dma((CHUNKS,)),
            dma((CHUNKS,)), dma((CHUNKS,)), dma((Z,)), dma((Z,)),
            dma((groups,)), dma((groups,)), dma((groups,)), dma((groups,)),
            dma((groups,)), dma((groups,)), dma((groups,)), dma((groups,)),
            dma((CHUNKS,)), dma((CHUNKS,)), dma((5,)),
        ],
        compiler_params=pltpu.CompilerParams(
            collective_id=0, has_side_effects=True, vmem_limit_bytes=45 * 1024 * 1024
        ),
    )(*inputs)


def shards(snapshots, cell_volume, mode_vectors, mode_scale, interp_weights):
    C, Z = lax.axis_size("cell"), lax.axis_size("narrow")
    rows, cols = snapshots.shape
    modes = mode_vectors.shape[1]
    fits = (
        C == 2 * Z == 8
        and C == 2 * CHUNKS
        and cols % (2 * 128 * CHUNKS) == 0
        and rows % (16 * Z) == 0
        and modes % (16 * C) == 0
        and interp_weights.shape[0] == rows == cols // 2
        and rows * cols <= 512 * 1024
        and interp_weights.shape[1] <= 1024
        and modes <= 512
    )
    run = shards_kernel if fits else shards_xla
    return run(snapshots, cell_volume, mode_vectors, mode_scale, interp_weights)


def solution(mesh):
    return jax.shard_map(
        shards,
        mesh=mesh,
        in_specs=(P("cell", "narrow"), P("cell"), P("narrow", None), P(), P("cell", "narrow")),
        out_specs=(P("cell", "narrow"), P("cell", "narrow")),
        check_vma=False,
    )
```

```python
import functools

import jax
import jax.numpy as jnp
from jax import lax
from jax.experimental import pallas as pl
from jax.experimental.pallas import tpu as pltpu
from jax.sharding import PartitionSpec as P

F32, BF16 = jnp.float32, jnp.bfloat16
MESH = pl.DeviceIdType.MESH
CHUNKS = 4
FAR = 4
EARLY = 2


def shards_xla(snapshots, cell_volume, mode_vectors, mode_scale, interp_weights):
    f32, bf16 = jnp.float32, jnp.bfloat16
    n_cell, n_narrow = lax.axis_size("cell"), lax.axis_size("narrow")
    total_cells = snapshots.shape[0] * n_cell
    rows = interp_weights.shape[0]
    weighted = (snapshots.astype(f32) * cell_volume[:, None]).astype(bf16)

    partial_shapes = jnp.dot(snapshots, mode_vectors, preferred_element_type=f32)
    mode_shapes = lax.psum(partial_shapes, "narrow").astype(bf16)

    gathered = lax.all_gather(snapshots, "narrow", axis=1, tiled=True)
    scaled_shapes = (
        mode_shapes.astype(f32) * (cell_volume / total_cells)[:, None] * mode_scale[None, :]
    ).astype(bf16)
    partial_coeffs = lax.dot_general(
        gathered, scaled_shapes, (((0,), (0,)), ((), ())), preferred_element_type=f32
    ).astype(bf16)
    coeffs = lax.psum_scatter(partial_coeffs, "cell", scatter_dimension=0, tiled=True)
    partial_new = lax.dot_general(
        coeffs, interp_weights, (((0,), (0,)), ((), ())), preferred_element_type=f32
    )
    new_coeffs = lax.psum(partial_new, "cell").astype(bf16)
    fields = jnp.dot(mode_shapes, new_coeffs, preferred_element_type=f32).astype(bf16)

    partial_gram = (
        lax.dot_general(gathered, weighted, (((0,), (0,)), ((), ())), preferred_element_type=f32)
        / total_cells
    ).astype(bf16)
    gram = lax.psum_scatter(partial_gram, "cell", scatter_dimension=0, tiled=True)
    return (gram.astype(f32), fields)


def pick(step, table, default):
    value = jnp.int32(default)
    for at, entry in table.items():
        value = jnp.where(step == at, jnp.int32(entry), value)
    return value


def kernel(
    C, Z, total, s_in, vrow_in, v_in, scale_in, w_in, gram, fields,
    s, vrow, v, scale, w, sg, sp, prow, vfull, wf, wfo, so, gsend, grecv, rrecv, gfar, ffar, frecv,
    mpart, msend, mout, mnear, mfar, mg, dm, csend, crecv, cown, kb, wq,
    nown, nsend, nrecv, ksend, krecv, kg,
    loc_sem, ps_sem, pr_sem, xs_sem, xr_sem, zs_sem, zr_sem, gs_sem, gr_sem, fs_sem, fr_sem,
    os_sem, or_sem, us_sem, ur_sem, hs_sem, hr_sem, m1s_sem, m1r_sem, m2s_sem, m2r_sem,
    cs_sem, cr_sem, bs_sem, br_sem, ws_sem, wr_sem, ks_sem, kr_sem, ls_sem, lr_sem, es_sem, er_sem, ds_sem, dr_sem, in_sem,
):
    c, z = lax.axis_index("cell"), lax.axis_index("narrow")
    groups = C // 2
    p, k = c // 2, c % 2
    mate = 2 * p + 1 - k
    rows, cols = s.shape
    modes = v.shape[1]
    half = cols // 2
    cw = half // CHUNKS
    mrows = rows // CHUNKS
    hm = modes // 2

    low = z < Z // 2
    out = jnp.where(low, 0, Z - 1)
    inner = jnp.where(low, 1, Z - 2)
    inner2 = Z - 1 - inner
    out2 = Z - 1 - out
    edge = z == out
    mid = z != out
    inward = jnp.where(edge, inner, inner2)

    def remote(src, dst, ssem, rsem, cell, narrow):
        return pltpu.make_async_remote_copy(
            src_ref=src, dst_ref=dst, send_sem=ssem, recv_sem=rsem,
            device_id={"cell": cell, "narrow": narrow}, device_id_type=MESH,
        )

    def rows_chip(h):
        q = pick(h, {0: 0, 1: 3, 2: 1, 3: 2}, 0)
        return jnp.where(low, groups - 1 - q, q)

    def chip(d):
        return (p + d) % groups

    def plane(d):
        return (z + d) % Z

    loads = [
        pltpu.make_async_copy(source, target, in_sem.at[at])
        for at, (source, target) in enumerate(
            ((s_in, s), (v_in, v), (vrow_in, vrow), (w_in, w), (scale_in, scale))
        )
    ]
    for load in loads:
        load.start()

    barrier = pltpu.get_barrier_semaphore()

    def greet(cell, narrow):
        pl.semaphore_signal(
            barrier, inc=1, device_id={"cell": cell, "narrow": narrow}, device_id_type=MESH
        )

    greet(mate, z)
    for d in range(1, groups):
        greet(2 * chip(d) + k, z)
    for d in range(1, Z):
        greet(c, plane(d))
    pl.semaphore_wait(barrier, groups + Z - 1)

    mine = pl.ds(pl.multiple_of(k * rows, rows), rows)
    theirs = pl.ds(pl.multiple_of((1 - k) * rows, rows), rows)

    def local_copy(h):
        lanes = pl.ds(pl.multiple_of(k * half + h * cw, cw), cw)
        return pltpu.make_async_copy(s.at[:, lanes], sg.at[z, h, mine], loc_sem.at[h])

    def mate_copy(h):
        lanes = pl.ds(pl.multiple_of((1 - k) * half + h * cw, cw), cw)
        return remote(s.at[:, lanes], sg.at[z, h, mine], ps_sem.at[h], pr_sem.at[h], mate, z)

    def w_rows(q):
        return pl.ds(pl.multiple_of(q * mrows, mrows), mrows)

    def w_send(q):
        return remote(w.at[w_rows(q)], wq.at[p], ws_sem.at[q], wr_sem.at[p], 2 * q + k, z)

    def w_recv(q):
        return remote(w.at[w_rows(q)], wq.at[q], ws_sem.at[q], wr_sem.at[q], 2 * q + k, z)

    def in_copy(b, h):
        return remote(sg.at[b, h], sg.at[b, h], zs_sem.at[0, b, h], zr_sem.at[b, h], c, inward)

    def out_copy(b, h):
        return remote(sg.at[b, h], sg.at[b, h], zs_sem.at[1, b, h], zr_sem.at[b, h], c, out)

    def m_near(q):
        return remote(msend.at[q], mnear.at[q], m1s_sem.at[q], m1r_sem.at[q], c, inward)

    def m_far(q):
        return remote(msend.at[q], mfar.at[q], m1s_sem.at[q], m2r_sem.at[q], c, inward)

    def m_out(q):
        return remote(mout.at[q], mfar.at[q], m2s_sem.at[q], m2r_sem.at[q], c, out)

    block_copy = remote(s, sp, xs_sem.at[0], xr_sem.at[0], mate, z)
    vol_copy = remote(vrow, prow, xs_sem.at[1], xr_sem.at[1], mate, z)
    new_half = remote(nsend, nrecv, xs_sem.at[2], xr_sem.at[2], mate, z)

    def d_rows(q):
        return pl.ds(pl.multiple_of(k * rows + q * mrows, mrows), mrows)

    def d_copy(q):
        return remote(dm.at[d_rows(q)], dm.at[d_rows(q)], ds_sem.at[q], dr_sem.at[q], mate, z)

    def shape(q, value):
        mg[q * mrows:(q + 1) * mrows, :] = value.astype(BF16)
        dm[d_rows(q), :] = (value * vfull[d_rows(q), :1]).astype(BF16)
        d_copy(q).start()

    loads[0].wait()
    for h in range(CHUNKS):
        local_copy(h).start()
        mate_copy(h).start()
    block_copy.start()
    loads[2].wait()
    vol_copy.start()
    loads[3].wait()
    for d in (1, 2, 3):
        w_send(chip(d)).start()

    loads[1].wait()
    mpart[...] = jnp.dot(s[...], v[...], preferred_element_type=F32).reshape(mpart.shape)

    loads[4].wait()

    @pl.when(edge)
    def _():
        for q in range(CHUNKS):
            msend[q] = mpart[q].astype(BF16)
            m_near(q).start()

    for h in range(CHUNKS):
        local_copy(h).wait()
        mate_copy(h).wait_recv()

        @pl.when(edge)
        def _():
            in_copy(z, h).start()

        if h == 0:
            @pl.when(mid)
            def _():
                in_copy(z, h).start()

        if h < 2:
            @pl.when(mid)
            def _():
                out_copy(z, h).start()

    def column(row):
        return jnp.broadcast_to(row[...], (128, rows)).T

    vfull[mine, :] = column(vrow)
    wf[mine, :] = (s[...].astype(F32) * vfull[mine, :1]).astype(BF16)
    vol_copy.wait_recv()
    vfull[theirs, :] = column(prow)
    block_copy.wait_recv()
    wf[theirs, :] = (sp[...].astype(F32) * vfull[theirs, :1]).astype(BF16)

    def apart(b):
        return jnp.where(p // 2 == b // 2, 0, 2) + jnp.where(p % 2 == b % 2, 0, 1)

    def flip(b, d):
        row = 1 - b // 2 if d == 2 else b // 2
        col = 1 - b % 2 if d == 1 else b % 2
        return 2 * row + col

    def direct(t, h, e, to):
        d = jnp.where(apart(to) == 1, 0, 1)
        r = jnp.where(t == FAR, CHUNKS, h)
        return remote(
            gsend.at[t, h, e], grecv.at[d, r, e], gs_sem.at[t, h, e], gr_sem.at[d, r, e],
            2 * to + k, z,
        )

    def across(t, h, e, to):
        return remote(
            gsend.at[t, h, e], rrecv.at[t, h], fs_sem.at[t, h, e], fr_sem.at[t, h],
            2 * flip(to, 1 if e == 0 else 2) + k, z,
        )

    def term(t, b, h, to, weights):
        value = lax.dot_general(
            sg[b, h], weights[...], (((0,), (0,)), ((), ())), preferred_element_type=F32
        ) * (1.0 / total)
        where = apart(to)

        @pl.when((where == 0) & (t != FAR))
        def _():
            gram[pl.ds(pl.multiple_of(h * cw, cw), cw), :] = value

        @pl.when((where == 0) & (t == FAR))
        def _():
            gfar[...] = value

        @pl.when(where != 0)
        def _():
            for e in range(2):
                gsend[t, h, e] = value[:, e * half:(e + 1) * half].astype(BF16)

        @pl.when(where == 3)
        def _():
            for e in range(2):
                across(t, h, e, to).start()

        @pl.when(where == 1)
        def _():
            direct(t, h, 1, to).start()

        @pl.when(where == 2)
        def _():
            direct(t, h, 0, to).start()

    def relay(t, h, to):
        where = apart(to)
        for e in range(2):
            @pl.when(where == e + 1)
            def _():
                across(t, h, e, to).wait_recv()
                gsend[t, h, e] = (
                    gsend[t, h, e].astype(F32) + rrecv[t, h].astype(F32)
                ).astype(BF16)
                direct(t, h, e, to).start()

    @pl.when(mid)
    def _():
        @pl.loop(0, EARLY)
        def _(h):
            term(z, z, h, z, wf)

    @pl.when(edge)
    def _():
        @pl.loop(0, 2)
        def _(h):
            in_copy(inner, h).wait_recv()
            term(inner, inner, h, inner, wf)

    def near(q):
        m_near(q).wait_recv()
        msend[q] = (mpart[q] + mnear[q].astype(F32)).astype(BF16)
        m_far(q).start()

    def far(q):
        m_out(q).wait_recv()
        value = mpart[q] + mfar[q].astype(F32)
        mout[q] = value.astype(BF16)
        m_out(q).start()
        shape(q, value + mnear[q].astype(F32))

    @pl.when(mid)
    def _():
        near(0)
        near(1)
        near(2)
        far(0)
        near(3)
        in_copy(z, 1).start()
        far(1)
        far(2)
        far(3)
        out_copy(z, 2).start()
        out_copy(z, 3).start()

    @pl.when(edge)
    def _():
        for q in range(CHUNKS):
            m_out(q).wait_recv()
            shape(q, mpart[q] + mfar[q].astype(F32))

    def o_copy(h):
        return remote(sg.at[out, h], so.at[h], os_sem.at[h], or_sem.at[h], mate, z)

    def o_weigh(block, h, core):
        lanes = pl.ds(pl.multiple_of(core * half + h * cw, cw), cw)
        wfo[:, lanes] = (block.astype(F32) * vfull[:, :1]).astype(BF16)

    def k_send(h):
        return remote(csend.at[h], crecv.at[p], cs_sem.at[h], cr_sem.at[p], 2 * h + k, z)

    def k_recv(q):
        return remote(csend.at[q], crecv.at[q], cs_sem.at[q], cr_sem.at[q], 2 * q + k, z)

    def k_share(t, b):
        return remote(kb.at[b], kb.at[b], bs_sem.at[t], br_sem.at[b], c, t)

    def n_send(q):
        return remote(ksend.at[q], krecv.at[p], ks_sem.at[q], kr_sem.at[p], 2 * q + k, z)

    def n_recv(q):
        return remote(ksend.at[q], krecv.at[q], ks_sem.at[q], kr_sem.at[q], 2 * q + k, z)

    def n_share(q, b):
        return remote(kg.at[k, b], kg.at[k, b], ls_sem.at[q], lr_sem.at[b], 2 * q + k, z)

    def n_mate(q, core):
        return remote(kg.at[core, q], kg.at[core, q], es_sem.at[q], er_sem.at[q], mate, z)

    def coefficients():
        for q in range(CHUNKS):
            d_copy(q).wait_recv()

        @pl.loop(0, CHUNKS)
        def _(h):
            value = lax.dot_general(
                sg[z, h], dm[...], (((0,), (0,)), ((), ())), preferred_element_type=F32
            )

            @pl.when(h == p)
            def _():
                cown[...] = value

            @pl.when(h != p)
            def _():
                csend[h] = value.astype(BF16)
                k_send(h).start()

    def coefficient_sum():
        value = cown[...]
        for d in (1, 2, 3):
            q = chip(d)
            k_recv(q).wait_recv()
            value = value + crecv[q].astype(F32)
        kb[z] = (value * (scale[...] * (1.0 / total))).astype(BF16)
        for d in (3, 2, 1):
            k_share(plane(d), z).start()

    def new_part():
        for d in (1, 2, 3):
            w_recv(chip(d)).wait_recv()
            k_share(plane(d), plane(d)).wait_recv()
        wq[p] = w[w_rows(p), :]
        value = lax.dot_general(
            kb[...].reshape(rows, modes), wq[...].reshape(rows, w.shape[1]),
            (((0,), (0,)), ((), ())), preferred_element_type=F32,
        )

        @pl.when(k == 0)
        def _():
            nown[...] = value[:hm]
            nsend[...] = value[hm:]

        @pl.when(k == 1)
        def _():
            nown[...] = value[hm:]
            nsend[...] = value[:hm]

        new_half.start()

    def new_scatter():
        new_half.wait_recv()
        value = nown[...] + nrecv[...]
        nown[...] = value
        ksend[...] = value.astype(BF16).reshape(ksend.shape)
        for d in (3, 1, 2):
            n_send(chip(d)).start()

    def new_sum():
        piece = hm // groups
        value = nown[pl.ds(pl.multiple_of(p * piece, piece), piece), :]
        for d in (1, 2, 3):
            q = chip(d)
            n_recv(q).wait_recv()
            value = value + krecv[q].astype(F32)
        kg[k, p] = value.astype(BF16)
        for d in (3, 1, 2):
            n_share(chip(d), p).start()
        n_mate(p, k).start()

    def new_gather():
        for d in (1, 2, 3):
            q = chip(d)
            n_share(q, q).wait_recv()
            n_mate(q, k).start()

    def reconstruct():
        for q in range(groups):
            n_mate(q, 1 - k).wait_recv()
        fields[...] = jnp.dot(
            mg[...], kg[...].reshape(modes, w.shape[1]), preferred_element_type=F32
        ).astype(BF16)

    own_rows = pick(jnp.where(low, groups - 1 - p, p), {0: 0, 3: 1, 1: 2, 2: 3}, 0)

    def far_send():
        return remote(ffar, frecv.at[own_rows], us_sem.at[0], ur_sem.at[own_rows], c, out)

    def far_share(q):
        return remote(frecv.at[q], frecv.at[q], hs_sem.at[0], ur_sem.at[q], 2 * out2 + k, z)

    def far_sum():
        value = gfar[...]
        for d in range(2):
            for e in range(2):
                to = flip(p, d + 1)
                remote(
                    gsend.at[FAR, 0, e], grecv.at[d, CHUNKS, e], gs_sem.at[FAR, 0, e],
                    gr_sem.at[d, CHUNKS, e], 2 * to + k, z,
                ).wait_recv()
        parts = [
            (grecv[0, CHUNKS, e].astype(F32) + grecv[1, CHUNKS, e].astype(F32)) for e in range(2)
        ]
        ffar[...] = (value + jnp.concatenate(parts, axis=1)).astype(BF16)
        far_send().start()

    OUT2, OUT, IN2, IN, ROWS = range(5)
    mid_terms = {
        0: (IN2, 0), 2: (OUT, 0), 3: (IN2, 1), 4: (OUT, 1), 5: (IN, 2), 6: (OUT2, 0), 7: (OUT, 2),
        8: (IN, 3), 9: (OUT, 3), 10: (OUT2, 1), 11: (ROWS, 0), 12: (ROWS, 1), 13: (OUT2, 2),
        14: (ROWS, 2), 16: (OUT2, 3), 17: (ROWS, 3), 18: (IN2, 2), 19: (IN2, 3),
    }
    mid_relays = {
        0: (IN, 0), 1: (IN, 1), 3: (IN2, 0), 5: (OUT, 0), 6: (IN2, 1), 7: (OUT, 1), 8: (IN, 2),
        10: (OUT2, 0), 11: (OUT, 2), 12: (OUT, 3), 13: (IN, 3), 14: (ROWS, 0), 15: (OUT2, 2),
        18: (ROWS, 2), 19: (ROWS, 3), 21: (IN2, 2),
    }
    mid_more = {13: (OUT2, 1), 14: (ROWS, 1), 19: (OUT2, 3), 21: (IN2, 3)}
    edge_terms = {
        2: (OUT, 0), 3: (OUT, 1), 4: (OUT, 2), 5: (OUT, 3), 6: (IN, 2), 7: (IN, 3), 10: (IN2, 0),
        14: (IN2, 1), 18: (IN2, 2), 20: (IN2, 3),
    }
    edge_relays = {
        2: (IN, 0), 3: (IN, 1), 5: (OUT, 0), 6: (OUT, 1), 7: (OUT, 2), 8: (OUT, 3), 9: (IN, 2),
        10: (IN, 3), 14: (IN2, 0), 16: (IN2, 1), 20: (IN2, 2), 21: (IN2, 3),
    }
    STEPS = 23

    def decode(step, for_mid, for_edge):
        def code(table):
            return {at: 4 * entry[0] + entry[1] for at, entry in table.items()}

        event = jnp.where(edge, pick(step, code(for_edge), -4), pick(step, code(for_mid), -4))
        kind, h = (event + 4) // 4 - 1, (event + 4) % 4
        b = jnp.where(
            kind == OUT, out, jnp.where(kind == IN2, inner2, jnp.where(kind == IN, inner, out2))
        )
        t = jnp.where(kind == ROWS, FAR, b)
        to = jnp.where(kind == ROWS, rows_chip(h), b)
        return kind, h, b, t, to

    def relay_step(step, for_mid, for_edge):
        kind, h, b, t, to = decode(step, for_mid, for_edge)

        @pl.when(kind >= 0)
        def _():
            relay(t, h, to)

    @pl.loop(0, STEPS)
    def _(step):
        kind, h, b, t, to = decode(step, mid_terms, edge_terms)

        @pl.when((kind >= 0) & (kind != ROWS))
        def _():
            @pl.when(b != z)
            def _():
                in_copy(b, h).wait_recv()

            @pl.when(mid & (kind == OUT))
            def _():
                in_copy(b, h).start()
                o_copy(h).start()

            @pl.when(mid & (kind == IN2))
            def _():
                out_copy(b, h).start()

            @pl.when(mid & (kind == OUT) & (h == CHUNKS - 1))
            def _():
                in_copy(z, 2).start()
                in_copy(z, 3).start()

            term(t, b, h, to, wf)

            @pl.when(mid & (kind == OUT))
            def _():
                o_weigh(sg[b, h], h, k)

        @pl.when(mid & (step == 11))
        def _():
            for q in range(CHUNKS):
                o_copy(q).wait_recv()
                o_weigh(so[q], q, 1 - k)

        @pl.when(kind == ROWS)
        def _():
            term(t, b, h, to, wfo)

        @pl.when(step == 1)
        def _():
            coefficients()

        @pl.when(step == 5)
        def _():
            coefficient_sum()

        @pl.when(step == 12)
        def _():
            new_part()

        @pl.when(step == 12)
        def _():
            new_scatter()

        @pl.when(step == 17)
        def _():
            new_sum()

        @pl.when(step == 22)
        def _():
            new_gather()

        relay_step(step, mid_relays, edge_relays)
        relay_step(step, mid_more, {})

        @pl.when(mid & (step == 19 + own_rows // 2))
        def _():
            far_sum()

        @pl.when(edge & (p != out2) & (step == STEPS - 2))
        def _():
            far_send().wait_recv()
            far_share(own_rows).start()

    reconstruct()

    @pl.when(mid | (p != out2))
    def _():
        @pl.loop(0, CHUNKS)
        def _(h):
            at = pl.ds(pl.multiple_of(h * cw, cw), cw)
            for d in range(2):
                to = flip(p, d + 1)
                for e in range(2):
                    remote(
                        gsend.at[p, h, e], grecv.at[d, h, e], gs_sem.at[p, h, e],
                        gr_sem.at[d, h, e], 2 * to + k, z,
                    ).wait_recv()
            for e in range(2):
                lanes = slice(e * half, (e + 1) * half)
                gram[at, lanes] = (
                    gram[at, lanes] + grecv[0, h, e].astype(F32) + grecv[1, h, e].astype(F32)
                )

    @pl.when(edge & (p == out2))
    def _():
        @pl.loop(0, CHUNKS)
        def _(h):
            remote(
                frecv.at[h], frecv.at[h], hs_sem.at[0], ur_sem.at[h], mate, z
            ).wait_recv()
            gram[pl.ds(pl.multiple_of(h * cw, cw), cw), :] = frecv[h].astype(F32)

    vol_copy.wait_send()
    block_copy.wait_send()
    new_half.wait_send()
    for h in range(CHUNKS):
        mate_copy(h).wait_send()
        m_near(h).wait_send()
        n_mate(h, k).wait_send()
        d_copy(h).wait_send()

        @pl.when(h != p)
        def _():
            k_send(h).wait_send()
    for d in (1, 2, 3):
        w_send(chip(d)).wait_send()
        n_send(chip(d)).wait_send()
        n_share(chip(d), p).wait_send()
        k_share(plane(d), z).wait_send()

    @pl.when(edge & (p != out2))
    def _():
        far_share(own_rows).wait_send()

    def sent(t, h, to):
        where = apart(to)

        @pl.when((where == 1) | (where == 2))
        def _():
            for e in range(2):
                direct(t, h, e, to).wait_send()

        @pl.when(where == 3)
        def _():
            for e in range(2):
                across(t, h, e, to).wait_send()

    @pl.loop(0, CHUNKS)
    def _(h):
        in_copy(z, h).wait_send()
        for b in range(Z):
            @pl.when(mid | (b != out2))
            def _():
                sent(b, h, b)

        @pl.when(mid)
        def _():
            in_copy(out, h).wait_send()
            out_copy(z, h).wait_send()
            out_copy(inner2, h).wait_send()
            m_out(h).wait_send()
            o_copy(h).wait_send()
            sent(FAR, h, rows_chip(h))

    @pl.when(mid)
    def _():
        far_send().wait_send()


def shards_kernel(snapshots, cell_volume, mode_vectors, mode_scale, interp_weights):
    C, Z = lax.axis_size("cell"), lax.axis_size("narrow")
    groups = C // 2
    rows, cols = snapshots.shape
    modes = mode_vectors.shape[1]
    conds = interp_weights.shape[1]
    half = cols // 2
    cw = half // CHUNKS
    mrows = rows // CHUNKS
    hm = modes // 2
    dma = pltpu.SemaphoreType.DMA
    vmem = pl.BlockSpec(memory_space=pltpu.VMEM)
    inputs = (snapshots, cell_volume[None, :], mode_vectors, mode_scale[None, :], interp_weights)
    inputs = [pltpu.with_memory_space_constraint(x, pltpu.HBM) for x in inputs]
    return pl.pallas_call(
        functools.partial(kernel, C, Z, rows * C),
        out_shape=(
            jax.ShapeDtypeStruct((half, cols), F32),
            jax.ShapeDtypeStruct((rows, conds), BF16),
        ),
        in_specs=[pl.BlockSpec(memory_space=pltpu.HBM)] * 5,
        out_specs=(vmem, vmem),
        scratch_shapes=[
            pltpu.VMEM((rows, cols), BF16),
            pltpu.VMEM((1, rows), F32),
            pltpu.VMEM((cols, modes), BF16),
            pltpu.VMEM((1, modes), F32),
            pltpu.VMEM((rows, conds), BF16),
            pltpu.VMEM((Z, CHUNKS, 2 * rows, cw), BF16),
            pltpu.VMEM((rows, cols), BF16),
            pltpu.VMEM((1, rows), F32),
            pltpu.VMEM((2 * rows, 128), F32),
            pltpu.VMEM((2 * rows, cols), BF16),
            pltpu.VMEM((2 * rows, cols), BF16),
            pltpu.VMEM((CHUNKS, 2 * rows, cw), BF16),
            pltpu.VMEM((FAR + 1, CHUNKS, 2, cw, half), BF16),
            pltpu.VMEM((2, CHUNKS + 1, 2, cw, half), BF16),
            pltpu.VMEM((FAR + 1, CHUNKS, cw, half), BF16),
            pltpu.VMEM((cw, cols), F32),
            pltpu.VMEM((cw, cols), BF16),
            pltpu.VMEM((CHUNKS, cw, cols), BF16),
            pltpu.VMEM((CHUNKS, mrows, modes), F32),
            pltpu.VMEM((CHUNKS, mrows, modes), BF16),
            pltpu.VMEM((CHUNKS, mrows, modes), BF16),
            pltpu.VMEM((CHUNKS, mrows, modes), BF16),
            pltpu.VMEM((CHUNKS, mrows, modes), BF16),
            pltpu.VMEM((rows, modes), BF16),
            pltpu.VMEM((2 * rows, modes), BF16),
            pltpu.VMEM((CHUNKS, cw, modes), BF16),
            pltpu.VMEM((CHUNKS, cw, modes), BF16),
            pltpu.VMEM((cw, modes), F32),
            pltpu.VMEM((Z, cw, modes), BF16),
            pltpu.VMEM((groups, mrows, conds), BF16),
            pltpu.VMEM((hm, conds), F32),
            pltpu.VMEM((hm, conds), F32),
            pltpu.VMEM((hm, conds), F32),
            pltpu.VMEM((groups, hm // groups, conds), BF16),
            pltpu.VMEM((groups, hm // groups, conds), BF16),
            pltpu.VMEM((2, groups, hm // groups, conds), BF16),
            dma((CHUNKS,)), dma((CHUNKS,)), dma((CHUNKS,)),
            dma((3,)), dma((3,)),
            dma((2, Z, CHUNKS)), dma((Z, CHUNKS)),
            dma((FAR + 1, CHUNKS, 2)), dma((2, CHUNKS + 1, 2)),
            dma((FAR + 1, CHUNKS, 2)), dma((FAR + 1, CHUNKS)),
            dma((CHUNKS,)), dma((CHUNKS,)),
            dma((1,)), dma((CHUNKS,)), dma((1,)), dma((1,)),
            dma((CHUNKS,)), dma((CHUNKS,)), dma((CHUNKS,)), dma((CHUNKS,)),
            dma((CHUNKS,)), dma((CHUNKS,)), dma((Z,)), dma((Z,)),
            dma((groups,)), dma((groups,)), dma((groups,)), dma((groups,)),
            dma((groups,)), dma((groups,)), dma((groups,)), dma((groups,)),
            dma((CHUNKS,)), dma((CHUNKS,)), dma((5,)),
        ],
        compiler_params=pltpu.CompilerParams(
            collective_id=0, has_side_effects=True, vmem_limit_bytes=45 * 1024 * 1024
        ),
    )(*inputs)


def shards(snapshots, cell_volume, mode_vectors, mode_scale, interp_weights):
    C, Z = lax.axis_size("cell"), lax.axis_size("narrow")
    rows, cols = snapshots.shape
    modes = mode_vectors.shape[1]
    fits = (
        C == 2 * Z == 8
        and C == 2 * CHUNKS
        and cols % (2 * 128 * CHUNKS) == 0
        and rows % (16 * Z) == 0
        and modes % (16 * C) == 0
        and interp_weights.shape[0] == rows == cols // 2
        and rows * cols <= 512 * 1024
        and interp_weights.shape[1] <= 1024
        and modes <= 512
    )
    run = shards_kernel if fits else shards_xla
    return run(snapshots, cell_volume, mode_vectors, mode_scale, interp_weights)


def solution(mesh):
    return jax.shard_map(
        shards,
        mesh=mesh,
        in_specs=(P("cell", "narrow"), P("cell"), P("narrow", None), P(), P("cell", "narrow")),
        out_specs=(P("cell", "narrow"), P("cell", "narrow")),
        check_vma=False,
    )
```
